512 devices in a mesh: seq: 64 (over y, z), piece: 8 (over x, core).
Axes of the slice: x: 4, y: 4, z: 16, core: 2. Of those that a mesh axis runs over, the one named last changes fastest.
Arguments:
- query: bfloat16 [8192, 2048], P('seq', 'piece'), may hold values from -64 to 64
- key_rows: bfloat16 [8192, 2048], P('seq', 'piece'), may hold values from -64 to 64
- value_matrix_rows: bfloat16 [8192, 2048], P('seq', 'piece'), may hold values from -6 to 6
- grad_out: bfloat16 [8192, 2048], P('seq', 'piece'), may hold values from -6 to 6
- rel_embed: bfloat16 [512, 64], replicated, may hold values from -6 to 6
Outputs:
- grad_query: bfloat16 [8192, 2048], P('seq', 'piece')
- grad_key: bfloat16 [8192, 2048], P('seq', 'piece')
- grad_value: bfloat16 [8192, 2048], P('seq', 'piece')
- grad_embed: float32 [512, 64], replicated
The draws below stay inside these ranges and needn't reach their ends.
All inputs are finite; a program needn't handle non-finite values.
Results may differ from the reference program's by a relative error of at most 0.0086.
Values may be sent and summed in bfloat16 or wider, within the bound.
No kernel may reach another device: no remote copies, remote signals or barrier semaphores. Data moves between devices by JAX's collectives and lax.ppermute only.
A program may use at most 64 MiB of HBM per device.

```python
import jax
import jax.numpy as jnp
from jax import lax

HEADS = 32
HEAD_DIM = 64
BAND_EXTENT = 512
TOK_DEV = 128
WIDTH = 2048
SEQ = 8192


def draw_query(key, part):
    base = jax.random.normal(jax.random.fold_in(key, 1), (SEQ, WIDTH), jnp.float32)
    return jnp.clip(base, -64.0, 64.0).astype(jnp.bfloat16)


def draw_key_rows(key, part):
    base = jax.random.normal(jax.random.fold_in(key, 2), (SEQ, WIDTH), jnp.float32)
    return jnp.clip(base, -64.0, 64.0).astype(jnp.bfloat16)


def block_levels(stream_key, extent, shards, least, largest):
    level, own = 1.0, jax.random.fold_in(stream_key, 6)
    for position, shards_of in shards:
        heights = jnp.exp(jax.random.uniform(jax.random.fold_in(own, position), (shards_of,), jnp.float32, least / len(shards), largest / len(shards)))
        level = level * jnp.repeat(heights, extent[position] // shards_of).reshape([-1 if axis == position else 1 for axis in range(len(extent))])
    return level


def scatter_about(own_key, shape, spread, most, split=(), kind=jnp.bfloat16):
    result = spread * jax.random.normal(own_key, shape, jnp.float32)
    if split:
        result = result * block_levels(own_key, shape, split, -0.22, 0.18)
    return jnp.clip(result, -most, most).astype(kind)


def setup_inputs(seed: int = 0) -> dict:
    key_list = jax.random.split(jax.random.key(seed), 6)
    return {
        "query": draw_query(jax.random.fold_in(key_list[5], 71), 0),
        "key_rows": draw_key_rows(jax.random.fold_in(key_list[5], 71), 0),
        "value_matrix_rows": scatter_about(key_list[2], (SEQ, WIDTH), 1.0, 6.0, ((0, 64), (1, 8))),
        "grad_out": scatter_about(key_list[3], (SEQ, WIDTH), 1.0, 6.0, ((0, 64), (1, 8))),
        "rel_embed": scatter_about(key_list[4], (BAND_EXTENT, HEAD_DIM), 1.0, 6.0),
    }


def skew_rel(along):
    head_count, row_tiles, cols = along.shape
    padded = jnp.pad(along, ((0, 0), (0, 0), (0, row_tiles)))
    flat = padded.reshape(head_count, row_tiles * (cols + row_tiles))[:, :row_tiles * (cols + row_tiles - 1)]
    return flat.reshape(head_count, row_tiles, cols + row_tiles - 1)[:, :, row_tiles:2 * row_tiles]

def unskew_rel(dscore, cols):
    zeros = jnp.zeros(dscore.shape[:2] + (cols,), dscore.dtype)
    _, pull = jax.vjp(skew_rel, zeros)
    return pull(dscore)[0]

def embed_slice(emb_pad, offset, row_tiles):
    return emb_pad[offset + 1:offset + 2 * row_tiles + 1][::-1]

def masked_scores(query, keys, slab, offset, present, scale):
    row_tiles = query.shape[0]
    qf = query.astype(jnp.float32)
    direct = jnp.einsum('thd,shd->hts', qf, keys.astype(jnp.float32))
    along = jnp.einsum('thd,rd->htr', qf, slab.astype(jnp.float32))
    score = scale * (direct + skew_rel(along))
    qpos = lax.broadcasted_iota(jnp.int32, (row_tiles, row_tiles), 0)
    kpos = lax.broadcasted_iota(jnp.int32, (row_tiles, row_tiles), 1)
    dist = offset + qpos - kpos
    valid = (dist >= 0) & (dist < BAND_EXTENT) & present
    return jnp.where(valid[None], score, -jnp.inf)

def pair_grads(prob, query, value_tensor, dout, delta, scale):
    prob_b = prob.astype(jnp.bfloat16)
    dprob = jnp.einsum('thd,shd->hts', dout.astype(jnp.float32), value_tensor.astype(jnp.float32))
    dscore = (prob * (dprob - delta[:, :, None]) * scale).astype(jnp.bfloat16)
    gkey = jnp.einsum('hts,thd->shd', dscore.astype(jnp.float32), query.astype(jnp.float32))
    gvalue = jnp.einsum('hts,thd->shd', prob_b.astype(jnp.float32), dout.astype(jnp.float32))
    return (dscore, gkey, gvalue)

def query_terms(dscore, keys, slab, query):
    dalong = unskew_rel(dscore, slab.shape[0]).astype(jnp.float32)
    dfloat = dscore.astype(jnp.float32)
    gquery = jnp.einsum('hts,shd->thd', dfloat, keys.astype(jnp.float32))
    gquery = gquery + jnp.einsum('htr,rd->thd', dalong, slab.astype(jnp.float32))
    gembed = jnp.einsum('htr,thd->rd', dalong, query.astype(jnp.float32))
    return (gquery, gembed)

def reference(query, key_rows, value_matrix_rows, grad_out, rel_embed):
    sequence_length, width = query.shape
    row_tiles = TOK_DEV
    head_count = HEADS
    head_feature_width = width // head_count
    scale = head_feature_width ** (-0.5)
    reach = BAND_EXTENT // row_tiles
    blocks = sequence_length // row_tiles
    qh = query.reshape(sequence_length, head_count, head_feature_width)
    doh = grad_out.reshape(sequence_length, head_count, head_feature_width)
    kpad = jnp.pad(key_rows.reshape(sequence_length, head_count, head_feature_width), ((BAND_EXTENT, 0), (0, 0), (0, 0)))
    value_padding = jnp.pad(value_matrix_rows.reshape(sequence_length, head_count, head_feature_width), ((BAND_EXTENT, 0), (0, 0), (0, 0)))
    emb_pad = jnp.pad(rel_embed, ((row_tiles, row_tiles + 1), (0, 0)))
    slabs = [embed_slice(emb_pad, step * row_tiles, row_tiles) for step in range(reach + 1)]

    def block_step(carry, index):
        gk_acc, gv_acc, ge_acc = carry
        start = (index * row_tiles).astype(jnp.int32)
        qb = lax.dynamic_slice_in_dim(qh, start, row_tiles, 0)
        dob = lax.dynamic_slice_in_dim(doh, start, row_tiles, 0)
        keys = []
        value_tensor = []
        scores = []
        for step in range(reach + 1):
            key_begin_index = (start - step * row_tiles + BAND_EXTENT).astype(jnp.int32)
            keys.append(lax.dynamic_slice_in_dim(kpad, key_begin_index, row_tiles, 0))
            value_tensor.append(lax.dynamic_slice_in_dim(value_padding, key_begin_index, row_tiles, 0))
            scores.append(masked_scores(qb, keys[step], slabs[step], step * row_tiles, index >= step, scale))
        top = scores[0].max(axis=2)
        for score in scores[1:]:
            top = jnp.maximum(top, score.max(axis=2))
        total = jnp.zeros_like(top)
        for score in scores:
            total = total + jnp.exp(score - top[:, :, None]).sum(axis=2)
        lse = top + jnp.log(total)
        probs = [jnp.exp(score - lse[:, :, None]) for score in scores]
        attn_out = jnp.zeros((row_tiles, head_count, head_feature_width), jnp.float32)
        for step in range(reach + 1):
            attn_out = attn_out + jnp.einsum('hts,shd->thd', probs[step].astype(jnp.bfloat16).astype(jnp.float32), value_tensor[step].astype(jnp.float32))
        delta = lax.optimization_barrier(jnp.sum(dob.astype(jnp.float32) * attn_out, axis=2)).T
        grad_q = jnp.zeros((row_tiles, head_count, head_feature_width), jnp.float32)
        for step in range(reach + 1):
            dscore, gkey, gvalue = pair_grads(probs[step], qb, value_tensor[step], dob, delta, scale)
            gquery, gembed = query_terms(dscore, keys[step], slabs[step], qb)
            grad_q = grad_q + gquery
            offset = step * row_tiles
            ge_acc = ge_acc.at[offset + 1:offset + 2 * row_tiles + 1].add(gembed[::-1])
            key_begin_index = (start - step * row_tiles + BAND_EXTENT).astype(jnp.int32)
            old_k = lax.dynamic_slice_in_dim(gk_acc, key_begin_index, row_tiles, 0)
            gk_acc = lax.dynamic_update_slice_in_dim(gk_acc, old_k + gkey, key_begin_index, 0)
            old_v = lax.dynamic_slice_in_dim(gv_acc, key_begin_index, row_tiles, 0)
            gv_acc = lax.dynamic_update_slice_in_dim(gv_acc, old_v + gvalue, key_begin_index, 0)
        return ((gk_acc, gv_acc, ge_acc), grad_q.astype(jnp.bfloat16))
    init = (jnp.zeros((sequence_length + BAND_EXTENT, head_count, head_feature_width), jnp.float32), jnp.zeros((sequence_length + BAND_EXTENT, head_count, head_feature_width), jnp.float32), jnp.zeros(emb_pad.shape, jnp.float32))
    (gk_acc, gv_acc, ge_acc), grad_q = lax.scan(block_step, init, jnp.arange(blocks, dtype=jnp.int32))
    grad_query = grad_q.reshape(sequence_length, width)
    grad_key = gk_acc[BAND_EXTENT:].reshape(sequence_length, width).astype(jnp.bfloat16)
    grad_value = gv_acc[BAND_EXTENT:].reshape(sequence_length, width).astype(jnp.bfloat16)
    return (grad_query, grad_key, grad_value, ge_acc[row_tiles:row_tiles + BAND_EXTENT])
```

```python
import jax
import jax.numpy as jnp
from jax import lax
from jax.experimental import pallas as pl
from jax.experimental.pallas import tpu as pltpu
from jax.sharding import PartitionSpec as P

HEAD_DIM = 64
BAND = 512
TOK = 128
GROUP = 4
ROWS = 256
SPAN = ROWS + BAND
DIMS = (4, 4, 4, 4, 2)
PIECES = 8
OTHERS = 16
F32 = jnp.float32
BF16 = jnp.bfloat16


def call(body, outs, *args, **kw):
    return pl.pallas_call(body, out_shape=[jax.ShapeDtypeStruct(s, d) for s, d in outs], **kw)(*args)


def mm(a, b, dims, precision=None):
    return lax.dot_general(a, b, (dims, ((), ())), precision=precision, preferred_element_type=F32)


NN = ((1,), (0,))
NT = ((1,), (1,))
TN = ((0,), (0,))


def flip_matrix(count, dtype):
    row = lax.broadcasted_iota(jnp.int32, (count, count), 0)
    col = lax.broadcasted_iota(jnp.int32, (count, count), 1)
    return jnp.where(row + col == count - 1, 1.0, 0.0).astype(dtype)


def pack_body(q, k, v, do, emb_t, packed, erev_t):
    for h in range(GROUP):
        cols = slice(h * HEAD_DIM, (h + 1) * HEAD_DIM)
        packed[h] = jnp.concatenate([q[:, cols], do[:, cols], k[:, cols], v[:, cols]], axis=1)
    flip = flip_matrix(TOK, BF16)
    blocks = BAND // TOK
    for b in range(blocks):
        cols = slice(b * TOK, (b + 1) * TOK)
        back = slice((blocks - 1 - b) * TOK, (blocks - b) * TOK)
        erev_t[:, back] = mm(emb_t[:, cols], flip, NN).astype(BF16)


def main_body(flag, own, halo, erev_t, ghalo, gown, gq_out, gemb, kv, gkv):
    scale = HEAD_DIM ** (-0.5)
    kv[:BAND] = halo[...].reshape(BAND, 2 * HEAD_DIM)
    own_all = own[...].reshape(BAND, 4 * HEAD_DIM)
    kv[BAND:] = own_all[:, 2 * HEAD_DIM :]
    emb_t = erev_t[...]
    flip = flip_matrix(ROWS, BF16)
    row = lax.broadcasted_iota(jnp.int32, (ROWS, SPAN), 0)
    col = lax.broadcasted_iota(jnp.int32, (ROWS, SPAN), 1)
    ahead = col - row - 1
    first = jnp.where(flag[0] > 0, 0, BAND)
    gerev = jnp.zeros((BAND, HEAD_DIM), F32)
    parts = []
    for b in range(BAND // ROWS):
        q = own_all[b * ROWS : (b + 1) * ROWS, :HEAD_DIM]
        do = own_all[b * ROWS : (b + 1) * ROWS, HEAD_DIM : 2 * HEAD_DIM]
        k = kv[b * ROWS : b * ROWS + SPAN, :HEAD_DIM]
        v = kv[b * ROWS : b * ROWS + SPAN, HEAD_DIM:]
        along = jnp.concatenate([mm(q, emb_t, NN), jnp.zeros((ROWS, SPAN - BAND), F32)], axis=1)
        along = pltpu.roll(along, 1, 1, stride=1, stride_axis=0)
        valid = (ahead >= 0) & (ahead < BAND) & (col + b * ROWS >= first)
        score = jnp.where(valid, scale * (mm(q, k, NT) + along), -jnp.inf)
        top = jnp.max(score, axis=1, keepdims=True)
        prob = jnp.exp(score - top)
        prob = prob * (1.0 / jnp.sum(prob, axis=1, keepdims=True))
        prob_b = prob.astype(BF16)
        dprob = mm(do, v, NT)
        delta = jnp.sum(prob_b.astype(F32) * dprob, axis=1, keepdims=True)
        dscore = (prob * (dprob - delta) * scale).astype(BF16)
        dalong = pltpu.roll(mm(flip, dscore, NN), SPAN - ROWS, 1, stride=1, stride_axis=0)
        dalong = dalong[:, :BAND].astype(BF16)
        gqe = mm(dalong, emb_t, NT)
        hi = gqe.astype(BF16)
        lo = (gqe - hi.astype(F32)).astype(BF16)
        gq = mm(dscore, k, NN) + mm(flip, hi, NN) + mm(flip, lo, NN)
        gq_out[b * ROWS : (b + 1) * ROWS] = gq
        gerev = gerev + mm(dalong, mm(flip, q, NN).astype(BF16), TN)
        parts.append(jnp.concatenate([mm(dscore, q, TN), mm(prob_b, do, TN)], axis=1))
    gkv[:ROWS] = parts[0][:ROWS]
    gkv[ROWS:SPAN] = parts[0][ROWS:] + parts[1][:BAND]
    gkv[SPAN:] = parts[1][BAND:]
    ghalo[...] = gkv[:BAND].astype(BF16).reshape(GROUP, TOK, 2 * HEAD_DIM)
    gown[...] = gkv[BAND:]
    for p in range(PIECES):
        chunk = gerev[BAND - (p + 1) * 64 : BAND - p * 64]
        gemb[p] = jnp.concatenate([chunk[:32], chunk[32:]], axis=1)


def sum_body(x, out):
    out[...] = jnp.sum(x[...].astype(F32), axis=0)


def out_pack_body(gown, gq, back, emb, out):
    gkv = gown[...].reshape(GROUP, TOK, 2 * HEAD_DIM) + back[...].astype(F32)
    gqs = gq[...].reshape(GROUP, TOK, HEAD_DIM)
    e = jnp.sum(emb[...], axis=0)
    e = jnp.concatenate([e[:, :HEAD_DIM], e[:, HEAD_DIM:]], axis=0)
    hi = e.astype(BF16)
    lo = (e - hi.astype(F32)).astype(BF16)
    hl = jnp.concatenate([hi, lo], axis=0)
    for g in range(GROUP):
        out[g] = jnp.concatenate([gkv[g].astype(BF16), gqs[g].astype(BF16), hl], axis=1)


def unpack_body(x, gq, gk, gv, emb):
    gk[...] = jnp.concatenate([x[h, :, :HEAD_DIM] for h in range(GROUP)], axis=1)
    gv[...] = jnp.concatenate([x[h, :, HEAD_DIM : 2 * HEAD_DIM] for h in range(GROUP)], axis=1)
    gq[...] = jnp.concatenate([x[h, :, 2 * HEAD_DIM : 3 * HEAD_DIM] for h in range(GROUP)], axis=1)
    hl = jnp.sum(x[:, :, 3 * HEAD_DIM :].astype(F32), axis=0)
    e = hl[:64] + hl[64:]
    e = jnp.concatenate([e[:32], e[32:]], axis=1)
    for i in range(emb.shape[0]):
        emb[i] = e


def last_body(x, out):
    e = jnp.sum(x[...].astype(F32), axis=0)
    e = jnp.concatenate([e[:, :HEAD_DIM], e[:, HEAD_DIM:]], axis=0)
    e = mm(flip_matrix(64, F32), e, NN, precision=lax.Precision.HIGHEST)
    e = jnp.concatenate([e[:32], e[32:]], axis=1)
    for i in range(PIECES):
        out[i] = e


def place_body(x, out):
    for p in range(PIECES):
        e = jnp.concatenate([x[p, :, :HEAD_DIM], x[p, :, HEAD_DIM:]], axis=0)
        out[:, p * 64 : (p + 1) * 64] = e.T


def local(query, key_rows, value_matrix_rows, grad_out, rel_embed):
    seq = ("y", "zg", "zi")
    piece = ("x", "core")
    here = lax.axis_index(seq)
    packed, erev_t = call(
        pack_body,
        [((GROUP, TOK, 4 * HEAD_DIM), BF16), ((HEAD_DIM, BAND), BF16)],
        query, key_rows, value_matrix_rows, grad_out, rel_embed.T,
    )
    own = lax.all_to_all(packed, "zi", 0, 0, tiled=True)
    n = lax.axis_size(seq)
    halo = lax.ppermute(own[:, :, 2 * HEAD_DIM :], seq, [(s, s + GROUP) for s in range(n - GROUP)])
    flag = (here >= GROUP).astype(jnp.int32).reshape(1)
    vm = pl.BlockSpec(memory_space=pltpu.VMEM)
    ghalo, gown, gq, gemb = call(
        main_body,
        [
            ((GROUP, TOK, 2 * HEAD_DIM), BF16),
            ((BAND, 2 * HEAD_DIM), F32),
            ((BAND, HEAD_DIM), F32),
            ((PIECES, 32, 128), F32),
        ],
        flag, own, halo, erev_t,
        in_specs=[pl.BlockSpec(memory_space=pltpu.SMEM), vm, vm, vm],
        scratch_shapes=[pltpu.VMEM((2 * BAND, 2 * HEAD_DIM), BF16), pltpu.VMEM((2 * BAND, 2 * HEAD_DIM), F32)],
    )
    back = lax.ppermute(ghalo, seq, [(s, s - GROUP) for s in range(GROUP, n)])
    gemb = lax.all_to_all(gemb, piece, 0, 0, tiled=True)
    (out,) = call(out_pack_body, [((GROUP, TOK, 4 * HEAD_DIM), BF16)], gown, gq, back, gemb)
    out = lax.all_to_all(out, "zi", 0, 0, tiled=True)
    grad_query, grad_key, grad_value, part = call(
        unpack_body,
        [((TOK, GROUP * HEAD_DIM), BF16)] * 3 + [((OTHERS, 32, 128), F32)],
        out,
    )
    part = lax.all_to_all(part, ("y", "zg"), 0, 0, tiled=True)
    (part,) = call(last_body, [((PIECES, 32, 128), F32)], part)
    part = lax.all_to_all(part, piece, 0, 0, tiled=True)
    (grad_embed_t,) = call(place_body, [((HEAD_DIM, BAND), F32)], part)
    return grad_query, grad_key, grad_value, grad_embed_t.T


def solution(mesh):
    fine = jax.sharding.Mesh(mesh.devices.reshape(DIMS), ("y", "zg", "zi", "x", "core"))
    rows = P(("y", "zg", "zi"), ("x", "core"))
    return jax.shard_map(
        local,
        mesh=fine,
        in_specs=(rows, rows, rows, rows, P()),
        out_specs=(rows, rows, rows, P()),
        check_vma=False,
    )
```

```python
import jax
import jax.numpy as jnp
from jax import lax
from jax.experimental import pallas as pl
from jax.experimental.pallas import tpu as pltpu
from jax.sharding import PartitionSpec as P


HEAD_DIM = 64
BAND = 512
TOK = 128
GROUP = 4
ROWS = 256
SPAN = ROWS + BAND
DIMS = (4, 4, 4, 4, 2)
BLOCKS = BAND // TOK
F32 = jnp.float32
BF16 = jnp.bfloat16


def call(body, outs, *args, **kw):
    args = [near(a) if a.ndim == 3 else a for a in args]
    shapes = [pltpu.VMEM(s, d) if v else jax.ShapeDtypeStruct(s, d) for s, d, v in outs]
    return pl.pallas_call(body, out_shape=shapes, **kw)(*args)


def near(x):
    return pltpu.with_memory_space_constraint(x, pltpu.VMEM)


def mm(a, b, dims, precision=None):
    return lax.dot_general(a, b, (dims, ((), ())), precision=precision, preferred_element_type=F32)


NN = ((1,), (0,))
NT = ((1,), (1,))
TN = ((0,), (0,))


def span(block):
    return slice(block * TOK, (block + 1) * TOK)


def flip_matrix(count, dtype):
    row = lax.broadcasted_iota(jnp.int32, (count, count), 0)
    col = lax.broadcasted_iota(jnp.int32, (count, count), 1)
    return jnp.where(row + col == count - 1, 1.0, 0.0).astype(dtype)


def pack_kv_body(k, v, packed):
    for h in range(GROUP):
        cols = slice(h * HEAD_DIM, (h + 1) * HEAD_DIM)
        packed[h] = jnp.concatenate([k[:, cols], v[:, cols]], axis=1)


def pack_q_body(q, do, emb_t, packed, erev_t):
    for h in range(GROUP):
        cols = slice(h * HEAD_DIM, (h + 1) * HEAD_DIM)
        packed[h] = jnp.concatenate([q[:, cols], do[:, cols]], axis=1)
    flip = flip_matrix(TOK, BF16)
    for b in range(BLOCKS):
        erev_t[:, span(BLOCKS - 1 - b)] = mm(emb_t[:, span(b)], flip, NN).astype(BF16)


def main_body(flag, qd, own, halo, erev_t, ghalo, gown, gq_out, gemb, kv, gkv):
    scale = HEAD_DIM ** (-0.5)
    kv[:BAND] = halo[...].reshape(BAND, 2 * HEAD_DIM)
    kv[BAND:] = own[...].reshape(BAND, 2 * HEAD_DIM)
    qdo = qd[...].reshape(BAND, 2 * HEAD_DIM)
    emb_t = erev_t[...]
    flip = flip_matrix(ROWS, BF16)
    row = lax.broadcasted_iota(jnp.int32, (ROWS, SPAN), 0)
    col = lax.broadcasted_iota(jnp.int32, (ROWS, SPAN), 1)
    ahead = col - row - 1
    first = jnp.where(flag[0] > 0, 0, BAND)
    gerev_t = jnp.zeros((HEAD_DIM, BAND), F32)
    parts = []
    for b in range(BAND // ROWS):
        q = qdo[b * ROWS : (b + 1) * ROWS, :HEAD_DIM]
        do = qdo[b * ROWS : (b + 1) * ROWS, HEAD_DIM:]
        k = kv[b * ROWS : b * ROWS + SPAN, :HEAD_DIM]
        v = kv[b * ROWS : b * ROWS + SPAN, HEAD_DIM:]
        along = jnp.concatenate([mm(q, emb_t, NN), jnp.zeros((ROWS, SPAN - BAND), F32)], axis=1)
        along = pltpu.roll(along, 1, 1, stride=1, stride_axis=0)
        valid = (ahead >= 0) & (ahead < BAND) & (col + b * ROWS >= first)
        score = jnp.where(valid, scale * (mm(q, k, NT) + along), -jnp.inf)
        top = jnp.max(score, axis=1, keepdims=True)
        prob = jnp.exp(score - top)
        prob = prob * (1.0 / jnp.sum(prob, axis=1, keepdims=True))
        prob_b = prob.astype(BF16)
        dprob = mm(do, v, NT)
        delta = jnp.sum(prob_b.astype(F32) * dprob, axis=1, keepdims=True)
        dscore = (prob * (dprob - delta) * scale).astype(BF16)
        dalong = pltpu.roll(mm(flip, dscore, NN), SPAN - ROWS, 1, stride=1, stride_axis=0)
        dalong = dalong[:, :BAND].astype(BF16)
        gqe = mm(dalong, emb_t, NT)
        hi = gqe.astype(BF16)
        lo = (gqe - hi.astype(F32)).astype(BF16)
        gq = mm(dscore, k, NN) + mm(flip, hi, NN) + mm(flip, lo, NN)
        gq_out[b * ROWS : (b + 1) * ROWS] = gq
        gerev_t = gerev_t + mm(mm(flip, q, NN).astype(BF16), dalong, TN)
        parts.append(jnp.concatenate([mm(dscore, q, TN), mm(prob_b, do, TN)], axis=1))
    gkv[:ROWS] = parts[0][:ROWS]
    gkv[ROWS:SPAN] = parts[0][ROWS:] + parts[1][:BAND]
    gkv[SPAN:] = parts[1][BAND:]
    ghalo[...] = gkv[:BAND].astype(BF16).reshape(GROUP, TOK, 2 * HEAD_DIM)
    gown[...] = gkv[BAND:]
    flip = flip_matrix(TOK, BF16)
    for b in range(BLOCKS):
        block = gerev_t[:, span(BLOCKS - 1 - b)]
        hi = block.astype(BF16)
        lo = (block - hi.astype(F32)).astype(BF16)
        block = mm(hi, flip, NN) + mm(lo, flip, NN)
        for d in range(HEAD_DIM // 8):
            gemb[d * BLOCKS + b] = block[d * 8 : (d + 1) * 8]


def out_pack_body(gown, gq, back, out):
    gkv = gown[...].reshape(GROUP, TOK, 2 * HEAD_DIM) + back[...].astype(F32)
    half = TOK // 2
    for g in range(GROUP):
        rows = gq[g * TOK : (g + 1) * TOK]
        out[g, :TOK] = gkv[g].astype(BF16)
        out[g, TOK:] = jnp.concatenate([rows[:half], rows[half:]], axis=1).astype(BF16)


def unpack_body(x, gq, gk, gv):
    half = TOK // 2
    gk[...] = jnp.concatenate([x[h, :TOK, :HEAD_DIM] for h in range(GROUP)], axis=1)
    gv[...] = jnp.concatenate([x[h, :TOK, HEAD_DIM:] for h in range(GROUP)], axis=1)
    gq[:half] = jnp.concatenate([x[h, TOK:, :HEAD_DIM] for h in range(GROUP)], axis=1)
    gq[half:] = jnp.concatenate([x[h, TOK:, HEAD_DIM:] for h in range(GROUP)], axis=1)


def local(query, key_rows, value_matrix_rows, grad_out, rel_embed):
    seq, line, plane = ("y", "zg", "zi"), ("zg", "zi"), ("y", "x", "core")
    n = lax.axis_size(seq)
    packed = ((GROUP, TOK, 2 * HEAD_DIM), BF16, True)
    (kv,) = call(pack_kv_body, [packed], key_rows, value_matrix_rows)
    kv = exchange(kv, "zi")
    halo = lax.ppermute(kv, seq, [(s, s + GROUP) for s in range(n - GROUP)])
    qd, erev_t = call(pack_q_body, [packed, ((HEAD_DIM, BAND), BF16, True)], query, grad_out, rel_embed.T)
    qd = exchange(qd, "zi")
    flag = (lax.axis_index(seq) >= GROUP).astype(jnp.int32).reshape(1)
    vm = pl.BlockSpec(memory_space=pltpu.VMEM)
    ghalo, gown, gq, gemb = call(
        main_body,
        [
            packed,
            ((BAND, 2 * HEAD_DIM), F32, True),
            ((BAND, HEAD_DIM), F32, True),
            ((lax.axis_size(plane), 8, 128), F32, True),
        ],
        flag, qd, kv, halo, near(erev_t),
        in_specs=[pl.BlockSpec(memory_space=pltpu.SMEM), vm, vm, vm, vm],
        scratch_shapes=[pltpu.VMEM((2 * BAND, 2 * HEAD_DIM), BF16), pltpu.VMEM((2 * BAND, 2 * HEAD_DIM), F32)],
    )
    back = lax.ppermute(ghalo, seq, [(s, s - GROUP) for s in range(GROUP, n)])
    part = jnp.sum(exchange(gemb, plane), axis=0)
    part = jnp.sum(spread(part, line), axis=0)
    whole = spread(part, plane)
    grad_embed_t = whole.reshape(8, BLOCKS, 8, 128).transpose(0, 2, 1, 3).reshape(HEAD_DIM, BAND)
    (out,) = call(out_pack_body, [((GROUP, TOK + TOK // 2, 2 * HEAD_DIM), BF16, True)], near(gown), near(gq), back)
    out = exchange(out, "zi")
    grad_query, grad_key, grad_value = call(unpack_body, [((TOK, GROUP * HEAD_DIM), BF16, False)] * 3, out)
    return grad_query, grad_key, grad_value, grad_embed_t.T


def exchange(x, axes):
    return lax.all_to_all(x, axes, 0, 0, tiled=True)


def spread(x, axes):
    return exchange(jnp.tile(x, (lax.axis_size(axes), 1, 1)), axes)


def solution(mesh):
    fine = jax.sharding.Mesh(mesh.devices.reshape(DIMS), ("y", "zg", "zi", "x", "core"))
    rows = P(("y", "zg", "zi"), ("x", "core"))
    return jax.shard_map(
        local,
        mesh=fine,
        in_specs=(rows, rows, rows, rows, P()),
        out_specs=(rows, rows, rows, P()),
        check_vma=False,
    )
```

```python
import jax
import jax.numpy as jnp
from jax import lax
from jax.experimental import pallas as pl
from jax.experimental.pallas import tpu as pltpu
from jax.sharding import PartitionSpec as P


HEAD_DIM = 64
BAND = 512
TOK = 128
GROUP = 4
ROWS = 256
SPAN = ROWS + BAND
DIMS = (4, 4, 4, 4, 2)
BLOCKS = BAND // TOK
F32 = jnp.float32
BF16 = jnp.bfloat16


def call(body, outs, *args, **kw):
    args = [near(a) if a.ndim == 3 else a for a in args]
    shapes = [pltpu.VMEM(s, d) if v else jax.ShapeDtypeStruct(s, d) for s, d, v in outs]
    return list(pl.pallas_call(body, out_shape=shapes, **kw)(*args))


def near(x):
    return pltpu.with_memory_space_constraint(x, pltpu.VMEM)


def mm(a, b, dims, precision=None):
    return lax.dot_general(a, b, (dims, ((), ())), precision=precision, preferred_element_type=F32)


NN = ((1,), (0,))
NT = ((1,), (1,))
TN = ((0,), (0,))


def span(block):
    return slice(block * TOK, (block + 1) * TOK)


def flip_matrix(count, dtype):
    row = lax.broadcasted_iota(jnp.int32, (count, count), 0)
    col = lax.broadcasted_iota(jnp.int32, (count, count), 1)
    return jnp.where(row + col == count - 1, 1.0, 0.0).astype(dtype)


def pack_kv_body(k, v, packed):
    for h in range(GROUP):
        cols = slice(h * HEAD_DIM, (h + 1) * HEAD_DIM)
        packed[h] = jnp.concatenate([k[:, cols], v[:, cols]], axis=1)


def pack_q_body(q, do, emb_t, packed, erev_t):
    for h in range(GROUP):
        cols = slice(h * HEAD_DIM, (h + 1) * HEAD_DIM)
        packed[h] = jnp.concatenate([q[:, cols], do[:, cols]], axis=1)
    flip = flip_matrix(TOK, BF16)
    for b in range(BLOCKS):
        erev_t[:, span(BLOCKS - 1 - b)] = mm(emb_t[:, span(b)], flip, NN).astype(BF16)


def main_body(flag, qd, own, halo, erev_t, ghalo, gown, gq_out, gemb, kv, gkv):
    scale = HEAD_DIM ** (-0.5)
    kv[:BAND] = halo[...].reshape(BAND, 2 * HEAD_DIM)
    kv[BAND:] = own[...].reshape(BAND, 2 * HEAD_DIM)
    qdo = qd[...].reshape(BAND, 2 * HEAD_DIM)
    emb_t = erev_t[...]
    flip = flip_matrix(ROWS, BF16)
    row = lax.broadcasted_iota(jnp.int32, (ROWS, SPAN), 0)
    col = lax.broadcasted_iota(jnp.int32, (ROWS, SPAN), 1)
    ahead = col - row - 1
    first = jnp.where(flag[0] > 0, 0, BAND)
    gerev_t = jnp.zeros((HEAD_DIM, BAND), F32)
    parts = []
    for b in range(BAND // ROWS):
        q = qdo[b * ROWS : (b + 1) * ROWS, :HEAD_DIM]
        do = qdo[b * ROWS : (b + 1) * ROWS, HEAD_DIM:]
        k = kv[b * ROWS : b * ROWS + SPAN, :HEAD_DIM]
        v = kv[b * ROWS : b * ROWS + SPAN, HEAD_DIM:]
        along = jnp.concatenate([mm(q, emb_t, NN), jnp.zeros((ROWS, SPAN - BAND), F32)], axis=1)
        along = pltpu.roll(along, 1, 1, stride=1, stride_axis=0)
        valid = (ahead >= 0) & (ahead < BAND) & (col + b * ROWS >= first)
        score = jnp.where(valid, scale * (mm(q, k, NT) + along), -jnp.inf)
        top = jnp.max(score, axis=1, keepdims=True)
        prob = jnp.exp(score - top)
        prob = prob * (1.0 / jnp.sum(prob, axis=1, keepdims=True))
        prob_b = prob.astype(BF16)
        dprob = mm(do, v, NT)
        delta = jnp.sum(prob_b.astype(F32) * dprob, axis=1, keepdims=True)
        dscore = (prob * (dprob - delta) * scale).astype(BF16)
        dalong = pltpu.roll(mm(flip, dscore, NN), SPAN - ROWS, 1, stride=1, stride_axis=0)
        dalong = dalong[:, :BAND].astype(BF16)
        gqe = mm(dalong, emb_t, NT)
        hi = gqe.astype(BF16)
        lo = (gqe - hi.astype(F32)).astype(BF16)
        gq = mm(dscore, k, NN) + mm(flip, hi, NN) + mm(flip, lo, NN)
        gq_out[b * ROWS : (b + 1) * ROWS] = gq
        gerev_t = gerev_t + mm(mm(flip, q, NN).astype(BF16), dalong, TN)
        parts.append(jnp.concatenate([mm(dscore, q, TN), mm(prob_b, do, TN)], axis=1))
    gkv[:ROWS] = parts[0][:ROWS]
    gkv[ROWS:SPAN] = parts[0][ROWS:] + parts[1][:BAND]
    gkv[SPAN:] = parts[1][BAND:]
    ghalo[...] = gkv[:BAND].astype(BF16).reshape(GROUP, TOK, 2 * HEAD_DIM)
    gown[...] = gkv[BAND:]
    flip = flip_matrix(TOK, BF16)
    for b in range(BLOCKS):
        block = gerev_t[:, span(BLOCKS - 1 - b)]
        hi = block.astype(BF16)
        lo = (block - hi.astype(F32)).astype(BF16)
        block = mm(hi, flip, NN) + mm(lo, flip, NN)
        for d in range(HEAD_DIM // 8):
            gemb[d * BLOCKS + b] = block[d * 8 : (d + 1) * 8]


def out_pack_body(place, gown, gq, back, *outs):
    half = TOK // 2
    for m, out in enumerate(outs):
        g = place[0] ^ m
        rows = pl.ds(pl.multiple_of(g * TOK, TOK), TOK)
        out[:TOK] = (gown[rows] + back[g].astype(F32)).astype(BF16)
        rows = gq[rows]
        out[TOK:] = jnp.concatenate([rows[:half], rows[half:]], axis=1).astype(BF16)


def unpack_body(place, x0, x1, x2, x3, gq, gk, gv, x):
    half = TOK // 2
    for m, part in enumerate((x0, x1, x2, x3)):
        x[place[0] ^ m] = part[...]
    gk[...] = jnp.concatenate([x[h, :TOK, :HEAD_DIM] for h in range(GROUP)], axis=1)
    gv[...] = jnp.concatenate([x[h, :TOK, HEAD_DIM:] for h in range(GROUP)], axis=1)
    gq[:half] = jnp.concatenate([x[h, TOK:, :HEAD_DIM] for h in range(GROUP)], axis=1)
    gq[half:] = jnp.concatenate([x[h, TOK:, HEAD_DIM:] for h in range(GROUP)], axis=1)


def local(query, key_rows, value_matrix_rows, grad_out, rel_embed):
    seq, line, plane = ("y", "zg", "zi"), ("zg", "zi"), ("y", "x", "core")
    n = lax.axis_size(seq)
    packed = ((GROUP, TOK, 2 * HEAD_DIM), BF16, True)
    (kv,) = call(pack_kv_body, [packed], key_rows, value_matrix_rows)
    kv = exchange(kv, "zi")
    halo = lax.ppermute(kv, seq, [(s, s + GROUP) for s in range(n - GROUP)])
    qd, erev_t = call(pack_q_body, [packed, ((HEAD_DIM, BAND), BF16, True)], query, grad_out, rel_embed.T)
    qd = exchange(qd, "zi")
    flag = (lax.axis_index(seq) >= GROUP).astype(jnp.int32).reshape(1)
    vm = pl.BlockSpec(memory_space=pltpu.VMEM)
    ghalo, gown, gq, gemb = call(
        main_body,
        [
            packed,
            ((BAND, 2 * HEAD_DIM), F32, True),
            ((BAND, HEAD_DIM), F32, True),
            ((lax.axis_size(plane), 8, 128), F32, True),
        ],
        flag, qd, kv, halo, near(erev_t),
        in_specs=[pl.BlockSpec(memory_space=pltpu.SMEM), vm, vm, vm, vm],
        scratch_shapes=[pltpu.VMEM((2 * BAND, 2 * HEAD_DIM), BF16), pltpu.VMEM((2 * BAND, 2 * HEAD_DIM), F32)],
    )
    back = lax.ppermute(ghalo, seq, [(s, s - GROUP) for s in range(GROUP, n)])
    part = jnp.sum(exchange(gemb, plane), axis=0)
    part = jnp.sum(spread(part, line), axis=0)
    whole = spread(part, plane)
    grad_embed_t = whole.reshape(8, BLOCKS, 8, 128).transpose(0, 2, 1, 3).reshape(HEAD_DIM, BAND)
    place = lax.axis_index("zi").reshape(1)
    slot = ((TOK + TOK // 2, 2 * HEAD_DIM), BF16, True)
    sm = pl.BlockSpec(memory_space=pltpu.SMEM)
    outs = call(out_pack_body, [slot] * GROUP, place, near(gown), near(gq), back, in_specs=[sm, vm, vm, vm])
    for m in range(1, GROUP):
        outs[m] = lax.ppermute(outs[m], seq, [(s, s ^ m) for s in range(n)])
    grad_query, grad_key, grad_value = call(
        unpack_body,
        [((TOK, GROUP * HEAD_DIM), BF16, False)] * 3,
        place, *[near(x) for x in outs],
        in_specs=[sm] + [vm] * GROUP,
        scratch_shapes=[pltpu.VMEM((GROUP, TOK + TOK // 2, 2 * HEAD_DIM), BF16)],
    )
    return grad_query, grad_key, grad_value, grad_embed_t.T


def exchange(x, axes):
    return lax.all_to_all(x, axes, 0, 0, tiled=True)


def spread(x, axes):
    return exchange(jnp.tile(x, (lax.axis_size(axes), 1, 1)), axes)


def solution(mesh):
    fine = jax.sharding.Mesh(mesh.devices.reshape(DIMS), ("y", "zg", "zi", "x", "core"))
    rows = P(("y", "zg", "zi"), ("x", "core"))
    return jax.shard_map(
        local,
        mesh=fine,
        in_specs=(rows, rows, rows, rows, P()),
        out_specs=(rows, rows, rows, P()),
        check_vma=False,
    )
```

```python
import jax
import jax.numpy as jnp
from jax import lax
from jax.experimental import pallas as pl
from jax.experimental.pallas import tpu as pltpu
from jax.sharding import PartitionSpec as P


HEAD_DIM = 64
BAND = 512
TOK = 128
REACH = BAND // TOK
SPAN = BAND + TOK
PAIR = 2 * HEAD_DIM
PAIRS = 2
ROWS = 2 * TOK
WIDE = PAIRS * PAIR
DIMS = (4, 4, 4, 4, 2)
SCALE = HEAD_DIM ** (-0.5)
F32 = jnp.float32
BF16 = jnp.bfloat16
NN = ((1,), (0,))
NT = ((1,), (1,))
TN = ((0,), (0,))


def call(body, outs, *args, **kw):
    shapes = [pltpu.VMEM(s, d) if v else jax.ShapeDtypeStruct(s, d) for s, d, v in outs]
    return list(pl.pallas_call(body, out_shape=shapes, **kw)(*args))


def near(x):
    return pltpu.with_memory_space_constraint(x, pltpu.VMEM)


def mm(a, b, dims):
    return lax.dot_general(a, b, (dims, ((), ())), preferred_element_type=F32)


def span(block):
    return slice(block * TOK, (block + 1) * TOK)


def flip_matrix(count):
    row = lax.broadcasted_iota(jnp.int32, (count, count), 0)
    col = lax.broadcasted_iota(jnp.int32, (count, count), 1)
    same = row // TOK == col // TOK
    return jnp.where(same & (row % TOK + col % TOK == TOK - 1), 1.0, 0.0).astype(BF16)


def skew(x, shift):
    halves = [pltpu.roll(x[span(b)], shift, 1, stride=1, stride_axis=0) for b in range(2)]
    return jnp.concatenate(halves, axis=0)


def stack_heads(x):
    low = lax.broadcasted_iota(jnp.int32, x.shape, 1) < HEAD_DIM
    zero = jnp.zeros_like(x)
    return jnp.concatenate([jnp.where(low, x, zero), jnp.where(low, zero, x)], axis=0)


def join_heads(x):
    low = lax.broadcasted_iota(jnp.int32, (TOK, PAIR), 1) < HEAD_DIM
    return jnp.where(low, x[:TOK], x[TOK:])


def early_body(q, do, emb_t, qs, dos, erev):
    flip = flip_matrix(TOK)
    for b in range(REACH):
        back = mm(emb_t[:, span(REACH - 1 - b)], flip, NN).astype(BF16)
        erev[:HEAD_DIM, span(b)] = back
        erev[HEAD_DIM:, span(b)] = back
    for p in range(PAIRS):
        lanes = slice(p * PAIR, (p + 1) * PAIR)
        qs[p] = stack_heads(q[:, lanes])
        dos[p] = stack_heads(do[:, lanes])


def main_body(first, qs, dos, erev, kv0, kv1, kv2, kv3, kv4, gq, far, d2, d1, d0, gemb):
    flip = flip_matrix(ROWS)
    row = lax.broadcasted_iota(jnp.int32, (ROWS, SPAN), 0) % TOK
    col = lax.broadcasted_iota(jnp.int32, (ROWS, SPAN), 1)
    ahead = col - row - 1
    valid = (ahead >= 0) & (ahead < BAND) & (col >= first[0])
    total = jnp.zeros((PAIR, BAND), F32)
    for p in range(PAIRS):
        k_lanes = slice(p * PAIR, (p + 1) * PAIR)
        v_lanes = slice(WIDE + p * PAIR, WIDE + (p + 1) * PAIR)
        blocks = (kv4, kv3, kv2, kv1, kv0)
        k = jnp.concatenate([x[:, k_lanes] for x in blocks], axis=0)
        v = jnp.concatenate([x[:, v_lanes] for x in blocks], axis=0)
        q, do = qs[p], dos[p]
        along = jnp.concatenate([mm(q, erev[...], NN), jnp.zeros((ROWS, TOK), F32)], axis=1)
        s = (skew(along, 1) + mm(q, k, NT)) * SCALE
        s = jnp.where(valid, s, -jnp.inf)
        dp = mm(do, v, NT)
        prob = jnp.exp(s - jnp.max(s, axis=1, keepdims=True))
        prob = prob * (1.0 / jnp.sum(prob, axis=1, keepdims=True))
        prob_b = prob.astype(BF16)
        delta = jnp.sum(prob_b.astype(F32) * dp, axis=1, keepdims=True)
        ds = (prob * (dp - delta) * SCALE).astype(BF16)
        dalong = skew(mm(flip, ds, NN), BAND)[:, :BAND].astype(BF16)
        total = total + mm(mm(flip, q, NN).astype(BF16), dalong, TN)
        for part, lanes in ((mm(ds, q, TN), k_lanes), (mm(prob_b, do, TN), v_lanes)):
            far[:TOK, lanes] = part[span(0)].astype(BF16)
            far[TOK:, lanes] = part[span(1)].astype(BF16)
            d2[:, lanes] = part[span(2)]
            d1[:, lanes] = part[span(3)]
            d0[:, lanes] = part[span(4)]
        gqe = mm(dalong, erev[...], NT)
        hi = gqe.astype(BF16)
        lo = (gqe - hi.astype(F32)).astype(BF16)
        g = mm(ds, k, NN) + mm(flip, hi, NN) + mm(flip, lo, NN)
        gq[:, k_lanes] = join_heads(g).astype(BF16)
    total = total[:HEAD_DIM] + total[HEAD_DIM:]
    flip = flip_matrix(TOK)
    for b in range(REACH):
        block = total[:, span(REACH - 1 - b)]
        hi = block.astype(BF16)
        lo = (block - hi.astype(F32)).astype(BF16)
        block = mm(hi, flip, NN) + mm(lo, flip, NN)
        for d in range(HEAD_DIM // 8):
            gemb[d * REACH + b] = block[d * 8 : (d + 1) * 8]


def add_body(far, d2, d1, e2, e1):
    e2[...] = (d2[...] + far[:TOK].astype(F32)).astype(BF16)
    e1[...] = (d1[...] + far[TOK:].astype(F32)).astype(BF16)


def last_body(d0, r2, r1, gk, gv):
    g = (d0[...] + r2[...].astype(F32) + r1[...].astype(F32)).astype(BF16)
    gk[...] = g[:, :WIDE]
    gv[...] = g[:, WIDE:]


def join_body(k, v, out):
    out[:, :WIDE] = k[...]
    out[:, WIDE:] = v[...]


SEQ = ("y", "zg", "zi")


def shift(x, steps):
    n = lax.axis_size(SEQ)
    return lax.ppermute(x, SEQ, [(s, s + steps) for s in range(max(0, -steps), min(n, n - steps))])


def exchange(x, axes):
    return lax.all_to_all(x, axes, 0, 0, tiled=True)


def spread(x, axes):
    return exchange(jnp.tile(x, (lax.axis_size(axes), 1, 1)), axes)


def local(query, key_rows, value_matrix_rows, grad_out, rel_embed):
    line, plane = ("zg", "zi"), ("y", "x", "core")
    block = (TOK, 2 * WIDE)
    (kv0,) = call(join_body, [(block, BF16, True)], key_rows, value_matrix_rows)
    kvs = [kv0]
    for _ in range(1, REACH + 1):
        kvs.append(shift(kvs[-1], 1))
    kvs = [near(x) for x in kvs]
    tall = (PAIRS, ROWS, PAIR)
    qs, dos, erev = call(
        early_body,
        [(tall, BF16, True), (tall, BF16, True), ((PAIR, BAND), BF16, True)],
        query, grad_out, rel_embed.T,
    )
    qs, dos = near(qs), near(dos)
    first = (TOK * jnp.maximum(REACH - lax.axis_index(SEQ), 0)).astype(jnp.int32).reshape(1)
    vm = pl.BlockSpec(memory_space=pltpu.VMEM)
    grad_query, far, d2, d1, d0, gemb = call(
        main_body,
        [((TOK, WIDE), BF16, False), ((2 * TOK, 2 * WIDE), BF16, True)]
        + [(block, F32, True)] * 3
        + [((lax.axis_size(plane), 8, 128), F32, True)],
        first, qs, dos, near(erev), *kvs,
        in_specs=[pl.BlockSpec(memory_space=pltpu.SMEM)] + [vm] * 8,
    )
    part = jnp.sum(exchange(gemb, plane), axis=0)
    part = jnp.sum(spread(part, line), axis=0)
    whole = spread(part, plane)
    grad_embed_t = whole.reshape(8, REACH, 8, 128).transpose(0, 2, 1, 3).reshape(HEAD_DIM, BAND)
    far = shift(far, -2)
    e2, e1 = call(add_body, [(block, BF16, True)] * 2, near(far), near(d2), near(d1))
    e2 = shift(e2, -2)
    e1 = shift(e1, -1)
    grad_key, grad_value = call(last_body, [((TOK, WIDE), BF16, False)] * 2, near(d0), near(e2), near(e1))
    return grad_query, grad_key, grad_value, grad_embed_t.T


def solution(mesh):
    fine = jax.sharding.Mesh(mesh.devices.reshape(DIMS), ("y", "zg", "zi", "x", "core"))
    rows = P(SEQ, ("x", "core"))
    return jax.shard_map(
        local,
        mesh=fine,
        in_specs=(rows, rows, rows, rows, P()),
        out_specs=(rows, rows, rows, P()),
        check_vma=False,
    )
```

```python
import jax
import jax.numpy as jnp
from jax import lax
from jax.experimental import pallas as pl
from jax.experimental.pallas import tpu as pltpu
from jax.sharding import PartitionSpec as P


HEAD_DIM = 64
BAND = 512
TOK = 128
REACH = BAND // TOK
HEADS = 2
PAIR = HEADS * HEAD_DIM
ROWS = 2 * TOK
SPAN = BAND + ROWS
DIMS = (4, 4, 4, 4, 2)
SCALE = HEAD_DIM ** (-0.5)
F32 = jnp.float32
BF16 = jnp.bfloat16
NN = ((1,), (0,))
NT = ((1,), (1,))
TN = ((0,), (0,))


def call(body, outs, *args, **kw):
    shapes = [pltpu.VMEM(s, d) if v else jax.ShapeDtypeStruct(s, d) for s, d, v in outs]
    return list(pl.pallas_call(body, out_shape=shapes, **kw)(*args))


def near(x):
    return pltpu.with_memory_space_constraint(x, pltpu.VMEM)


def mm(a, b, dims):
    return lax.dot_general(a, b, (dims, ((), ())), preferred_element_type=F32)


def span(block):
    return slice(block * TOK, (block + 1) * TOK)


def flip_matrix(count):
    row = lax.broadcasted_iota(jnp.int32, (count, count), 0)
    col = lax.broadcasted_iota(jnp.int32, (count, count), 1)
    return jnp.where(row + col == count - 1, 1.0, 0.0).astype(BF16)


def low_lanes(shape):
    return lax.broadcasted_iota(jnp.int32, shape, len(shape) - 1) < HEAD_DIM


def half(b):
    return pl.ds(pl.multiple_of(b * TOK, TOK), TOK)


def pack_body(odd, x, y, keep, send):
    take = odd[0] > 0
    for i, a in enumerate((x, y)):
        lanes = slice(i * PAIR, (i + 1) * PAIR)
        keep[:, lanes] = jnp.where(take, a[:, PAIR:], a[:, :PAIR])
        send[:, lanes] = jnp.where(take, a[:, :PAIR], a[:, PAIR:])


def pack_q_body(odd, x, y, emb_t, keep, send, erev):
    pack_body(odd, x, y, keep, send)
    flip = flip_matrix(TOK)
    for b in range(REACH):
        back = mm(emb_t[:, span(REACH - 1 - b)], flip, NN).astype(BF16)
        erev[:HEAD_DIM, span(b)] = back
        erev[HEAD_DIM:, span(b)] = back


def unite_body(odd, keep, got, out):
    out[half(odd[0])] = keep[...]
    out[half(1 - odd[0])] = got[...]


def unite_q_body(odd, keep, got, qs, dos):
    low = low_lanes((TOK, PAIR))
    zero = jnp.zeros((TOK, PAIR), BF16)
    for rows, part in ((half(odd[0]), keep), (half(1 - odd[0]), got)):
        for i, out in enumerate((qs, dos)):
            x = part[:, i * PAIR : (i + 1) * PAIR]
            out[0, rows] = jnp.where(low, x, zero)
            out[1, rows] = jnp.where(low, zero, x)


def main_body(first, qs, dos, erev, kv2, kv1, kv0, gq, far, d1, d0, gemb):
    flip = flip_matrix(ROWS)
    row = lax.broadcasted_iota(jnp.int32, (ROWS, SPAN), 0)
    col = lax.broadcasted_iota(jnp.int32, (ROWS, SPAN), 1)
    ahead = col - row - 1
    valid = (ahead >= 0) & (ahead < BAND) & (col >= first[0])
    k = jnp.concatenate([x[:, :PAIR] for x in (kv2, kv1, kv0)], axis=0)
    v = jnp.concatenate([x[:, PAIR:] for x in (kv2, kv1, kv0)], axis=0)
    total = jnp.zeros((PAIR, BAND), F32)
    gk = jnp.zeros((SPAN, PAIR), F32)
    gv = jnp.zeros((SPAN, PAIR), F32)
    gqs = []
    for h in range(HEADS):
        q, do = qs[h], dos[h]
        along = jnp.concatenate([mm(q, erev[...], NN), jnp.zeros((ROWS, ROWS), F32)], axis=1)
        s = (pltpu.roll(along, 1, 1, stride=1, stride_axis=0) + mm(q, k, NT)) * SCALE
        s = jnp.where(valid, s, -jnp.inf)
        dp = mm(do, v, NT)
        prob = jnp.exp(s - jnp.max(s, axis=1, keepdims=True))
        prob = prob * (1.0 / jnp.sum(prob, axis=1, keepdims=True))
        prob_b = prob.astype(BF16)
        delta = jnp.sum(prob_b.astype(F32) * dp, axis=1, keepdims=True)
        ds = (prob * (dp - delta) * SCALE).astype(BF16)
        dalong = pltpu.roll(mm(flip, ds, NN), BAND, 1, stride=1, stride_axis=0)[:, :BAND].astype(BF16)
        total = total + mm(mm(flip, q, NN).astype(BF16), dalong, TN)
        gk = gk + mm(ds, q, TN)
        gv = gv + mm(prob_b, do, TN)
        gqe = mm(dalong, erev[...], NT)
        hi = gqe.astype(BF16)
        lo = (gqe - hi.astype(F32)).astype(BF16)
        gqs.append(mm(ds, k, NN) + mm(flip, hi, NN) + mm(flip, lo, NN))
    gq[...] = jnp.where(low_lanes((ROWS, PAIR)), *gqs).astype(BF16)
    for part, lanes in ((gk, slice(0, PAIR)), (gv, slice(PAIR, 2 * PAIR))):
        far[:, lanes] = part[:ROWS].astype(BF16)
        d1[:, lanes] = part[ROWS : 2 * ROWS]
        d0[:, lanes] = part[2 * ROWS :]
    total = total[:HEAD_DIM] + total[HEAD_DIM:]
    flip = flip_matrix(TOK)
    for b in range(REACH):
        block = total[:, span(REACH - 1 - b)]
        hi = block.astype(BF16)
        lo = (block - hi.astype(F32)).astype(BF16)
        block = mm(hi, flip, NN) + mm(lo, flip, NN)
        for d in range(HEAD_DIM // 8):
            gemb[d * REACH + b] = block[d * 8 : (d + 1) * 8]


def add_body(far, d1, out):
    out[...] = (d1[...] + far[...].astype(F32)).astype(BF16)


def final_body(odd, got, d0, gq, keep, send):
    for rows, out in ((half(odd[0]), keep), (half(1 - odd[0]), send)):
        out[:, :PAIR] = gq[rows]
        out[:, PAIR:] = (d0[rows] + got[rows].astype(F32)).astype(BF16)


def unpack_body(odd, keep, got, *outs):
    swap = odd[0] > 0
    for i, out in enumerate(outs):
        lanes = slice(i * PAIR, (i + 1) * PAIR)
        a, b = keep[:, lanes], got[:, lanes]
        out[:, :PAIR] = jnp.where(swap, b, a)
        out[:, PAIR:] = jnp.where(swap, a, b)


SEQ = ("y", "zg", "zi")


def shift(x, steps):
    n = lax.axis_size(SEQ)
    return lax.ppermute(x, SEQ, [(s, s + steps) for s in range(max(0, -steps), min(n, n - steps))])


def exchange(x, axes):
    return lax.all_to_all(x, axes, 0, 0, tiled=True)


def spread(x, axes):
    return exchange(jnp.tile(x, (lax.axis_size(axes), 1, 1)), axes)


def swap(x):
    return lax.ppermute(x, SEQ, [(s, s ^ 1) for s in range(lax.axis_size(SEQ))])


def local(query, key_rows, value_matrix_rows, grad_out, rel_embed):
    line, plane = ("zg", "zi"), ("y", "x", "core")
    here = lax.axis_index(SEQ)
    odd = (here % 2).reshape(1)
    sm, vm = pl.BlockSpec(memory_space=pltpu.SMEM), pl.BlockSpec(memory_space=pltpu.VMEM)

    def staged_call(body, outs, *args):
        return call(body, outs, *args, in_specs=[sm] + [vm] * (len(args) - 1))

    part = ((TOK, 2 * PAIR), BF16, True)
    keep, send = staged_call(pack_body, [part] * 2, odd, key_rows, value_matrix_rows)
    got = swap(send)
    unit = (ROWS, 2 * PAIR)
    (kv0,) = staged_call(unite_body, [(unit, BF16, True)], odd, near(keep), near(got))
    kv1 = shift(kv0, 2)
    kv2 = shift(kv1, 2)
    keep, send, erev = staged_call(
        pack_q_body, [part, part, ((PAIR, BAND), BF16, True)], odd, query, grad_out, rel_embed.T
    )
    got = swap(send)
    heads = ((HEADS, ROWS, PAIR), BF16, True)
    qs, dos = staged_call(unite_q_body, [heads] * 2, odd, near(keep), near(got))
    first = (ROWS * jnp.maximum(BAND // ROWS - here // 2, 0)).astype(jnp.int32).reshape(1)
    gq, far, d1, d0, gemb = staged_call(
        main_body,
        [((ROWS, PAIR), BF16, True), (unit, BF16, True), (unit, F32, True), (unit, F32, True)]
        + [((lax.axis_size(plane), 8, 128), F32, True)],
        first, near(qs), near(dos), near(erev), near(kv2), near(kv1), near(kv0),
    )
    part = jnp.sum(exchange(gemb, plane), axis=0)
    part = jnp.sum(spread(part, line), axis=0)
    whole = spread(part, plane)
    grad_embed_t = whole.reshape(8, REACH, 8, 128).transpose(0, 2, 1, 3).reshape(HEAD_DIM, BAND)
    far = shift(far, -2)
    (far,) = call(add_body, [(unit, BF16, True)], near(far), near(d1))
    far = shift(far, -2)
    third = ((TOK, 3 * PAIR), BF16, True)
    keep, send = staged_call(final_body, [third] * 2, odd, near(far), near(d0), near(gq))
    got = swap(send)
    grads = staged_call(unpack_body, [((TOK, 2 * PAIR), BF16, False)] * 3, odd, near(keep), near(got))
    return (*grads, grad_embed_t.T)


def solution(mesh):
    fine = jax.sharding.Mesh(mesh.devices.reshape(DIMS), ("y", "zg", "zi", "x", "core"))
    rows = P(SEQ, ("x", "core"))
    return jax.shard_map(
        local,
        mesh=fine,
        in_specs=(rows, rows, rows, rows, P()),
        out_specs=(rows, rows, rows, P()),
        check_vma=False,
    )
```

```python
import jax
import jax.numpy as jnp
from jax import lax
from jax.experimental import pallas as pl
from jax.experimental.pallas import tpu as pltpu
from jax.sharding import PartitionSpec as P


HEAD_DIM = 64
BAND = 512
TOK = 128
REACH = BAND // TOK
HEADS = 2
PAIR = HEADS * HEAD_DIM
ROWS = 2 * TOK
SPAN = BAND + ROWS
DIMS = (4, 4, 4, 4, 2)
SCALE = HEAD_DIM ** (-0.5)
F32 = jnp.float32
BF16 = jnp.bfloat16
NN = ((1,), (0,))
NT = ((1,), (1,))
TN = ((0,), (0,))


def call(body, outs, *args, **kw):
    shapes = [pltpu.VMEM(s, d) if v else jax.ShapeDtypeStruct(s, d) for s, d, v in outs]
    return list(pl.pallas_call(body, out_shape=shapes, **kw)(*args))


def near(x):
    return pltpu.with_memory_space_constraint(x, pltpu.VMEM)


def mm(a, b, dims):
    return lax.dot_general(a, b, (dims, ((), ())), preferred_element_type=F32)


def span(block):
    return slice(block * TOK, (block + 1) * TOK)


def flip_matrix(count):
    row = lax.broadcasted_iota(jnp.int32, (count, count), 0)
    col = lax.broadcasted_iota(jnp.int32, (count, count), 1)
    return jnp.where(row + col == count - 1, 1.0, 0.0).astype(BF16)


def low_lanes(shape):
    return lax.broadcasted_iota(jnp.int32, shape, len(shape) - 1) < HEAD_DIM


def half(b):
    return pl.ds(pl.multiple_of(b * TOK, TOK), TOK)


def pack_body(odd, x, y, keep, send):
    take = odd[0] > 0
    for i, a in enumerate((x, y)):
        lanes = slice(i * PAIR, (i + 1) * PAIR)
        keep[:, lanes] = jnp.where(take, a[:, PAIR:], a[:, :PAIR])
        send[:, lanes] = jnp.where(take, a[:, :PAIR], a[:, PAIR:])


def pack_q_body(odd, x, y, emb_t, keep, send, erev):
    pack_body(odd, x, y, keep, send)
    flip = flip_matrix(TOK)
    for b in range(REACH):
        back = mm(emb_t[:, span(REACH - 1 - b)], flip, NN).astype(BF16)
        erev[:HEAD_DIM, span(b)] = back
        erev[HEAD_DIM:, span(b)] = back


def unite_body(odd, keep, got, out):
    out[half(odd[0])] = keep[...]
    out[half(1 - odd[0])] = got[...]


def unite_q_body(odd, keep, got, qs, dos):
    low = low_lanes((TOK, PAIR))
    zero = jnp.zeros((TOK, PAIR), BF16)
    for rows, part in ((half(odd[0]), keep), (half(1 - odd[0]), got)):
        for i, out in enumerate((qs, dos)):
            x = part[:, i * PAIR : (i + 1) * PAIR]
            out[0, rows] = jnp.where(low, x, zero)
            out[1, rows] = jnp.where(low, zero, x)


def main_body(first, qs, dos, erev, kv2, kv1, kv0, gq, far, d1, d0, gemb):
    flip = flip_matrix(ROWS)
    row = lax.broadcasted_iota(jnp.int32, (ROWS, SPAN), 0)
    col = lax.broadcasted_iota(jnp.int32, (ROWS, SPAN), 1)
    ahead = col - row - 1
    valid = (ahead >= 0) & (ahead < BAND) & (col >= first[0])
    k = jnp.concatenate([x[:, :PAIR] for x in (kv2, kv1, kv0)], axis=0)
    v = jnp.concatenate([x[:, PAIR:] for x in (kv2, kv1, kv0)], axis=0)
    total = jnp.zeros((PAIR, BAND), F32)
    gk = jnp.zeros((SPAN, PAIR), F32)
    gv = jnp.zeros((SPAN, PAIR), F32)
    gqs = []
    for h in range(HEADS):
        q, do = qs[h], dos[h]
        along = jnp.concatenate([mm(q, erev[...], NN), jnp.zeros((ROWS, ROWS), F32)], axis=1)
        s = (pltpu.roll(along, 1, 1, stride=1, stride_axis=0) + mm(q, k, NT)) * SCALE
        s = jnp.where(valid, s, -jnp.inf)
        dp = mm(do, v, NT)
        prob = jnp.exp(s - jnp.max(s, axis=1, keepdims=True))
        prob = prob * (1.0 / jnp.sum(prob, axis=1, keepdims=True))
        prob_b = prob.astype(BF16)
        delta = jnp.sum(prob_b.astype(F32) * dp, axis=1, keepdims=True)
        ds = (prob * (dp - delta) * SCALE).astype(BF16)
        dalong = pltpu.roll(mm(flip, ds, NN), BAND, 1, stride=1, stride_axis=0)[:, :BAND].astype(BF16)
        total = total + mm(mm(flip, q, NN).astype(BF16), dalong, TN)
        gk = gk + mm(ds, q, TN)
        gv = gv + mm(prob_b, do, TN)
        gqe = mm(dalong, erev[...], NT)
        hi = gqe.astype(BF16)
        lo = (gqe - hi.astype(F32)).astype(BF16)
        gqs.append(mm(ds, k, NN) + mm(flip, hi, NN) + mm(flip, lo, NN))
    gq[...] = jnp.where(low_lanes((ROWS, PAIR)), *gqs).astype(BF16)
    for part, lanes in ((gk, slice(0, PAIR)), (gv, slice(PAIR, 2 * PAIR))):
        far[:, lanes] = part[:ROWS].astype(BF16)
        d1[:, lanes] = part[ROWS : 2 * ROWS]
        d0[:, lanes] = part[2 * ROWS :]
    total = total[:HEAD_DIM] + total[HEAD_DIM:]
    flip = flip_matrix(TOK)
    for b in range(REACH):
        block = total[:, span(REACH - 1 - b)]
        hi = block.astype(BF16)
        lo = (block - hi.astype(F32)).astype(BF16)
        block = mm(hi, flip, NN) + mm(lo, flip, NN)
        for d in range(HEAD_DIM // 8):
            gemb[d * REACH + b] = block[d * 8 : (d + 1) * 8]


def sum_body(x, out):
    out[...] = jnp.broadcast_to(jnp.sum(x[...], axis=0, keepdims=True), out.shape)


def add_body(far, d1, out):
    out[...] = (d1[...] + far[...].astype(F32)).astype(BF16)


def final_body(odd, got, d0, gq, keep, send):
    for rows, out in ((half(odd[0]), keep), (half(1 - odd[0]), send)):
        out[:, :PAIR] = gq[rows]
        out[:, PAIR:] = (d0[rows] + got[rows].astype(F32)).astype(BF16)


def unpack_body(odd, keep, got, *outs):
    swap = odd[0] > 0
    for i, out in enumerate(outs):
        lanes = slice(i * PAIR, (i + 1) * PAIR)
        a, b = keep[:, lanes], got[:, lanes]
        out[:, :PAIR] = jnp.where(swap, b, a)
        out[:, PAIR:] = jnp.where(swap, a, b)


SEQ = ("y", "zg", "zi")


def shift(x, steps):
    n = lax.axis_size(SEQ)
    return lax.ppermute(x, SEQ, [(s, s + steps) for s in range(max(0, -steps), min(n, n - steps))])


def exchange(x, axes):
    return lax.all_to_all(x, axes, 0, 0, tiled=True)


def swap(x):
    return lax.ppermute(x, SEQ, [(s, s ^ 1) for s in range(lax.axis_size(SEQ))])


def local(query, key_rows, value_matrix_rows, grad_out, rel_embed):
    line, plane = ("zg", "zi"), ("y", "x", "core")
    here = lax.axis_index(SEQ)
    odd = (here % 2).reshape(1)
    sm, vm = pl.BlockSpec(memory_space=pltpu.SMEM), pl.BlockSpec(memory_space=pltpu.VMEM)

    def staged_call(body, outs, *args):
        return call(body, outs, *args, in_specs=[sm] + [vm] * (len(args) - 1))

    part = ((TOK, 2 * PAIR), BF16, True)
    keep, send = staged_call(pack_body, [part] * 2, odd, key_rows, value_matrix_rows)
    got = swap(send)
    unit = (ROWS, 2 * PAIR)
    (kv0,) = staged_call(unite_body, [(unit, BF16, True)], odd, near(keep), near(got))
    kv1 = shift(kv0, 2)
    kv2 = shift(kv1, 2)
    keep, send, erev = staged_call(
        pack_q_body, [part, part, ((PAIR, BAND), BF16, True)], odd, query, grad_out, rel_embed.T
    )
    got = swap(send)
    heads = ((HEADS, ROWS, PAIR), BF16, True)
    qs, dos = staged_call(unite_q_body, [heads] * 2, odd, near(keep), near(got))
    first = (ROWS * jnp.maximum(BAND // ROWS - here // 2, 0)).astype(jnp.int32).reshape(1)
    gq, far, d1, d0, gemb = staged_call(
        main_body,
        [((ROWS, PAIR), BF16, True), (unit, BF16, True), (unit, F32, True), (unit, F32, True)]
        + [((lax.axis_size(plane), 8, 128), F32, True)],
        first, near(qs), near(dos), near(erev), near(kv2), near(kv1), near(kv0),
    )
    whole = exchange(gemb, plane)
    for axes in (line, plane):
        tiles = ((lax.axis_size(axes), 8, 128), F32, True)
        (whole,) = call(sum_body, [tiles], near(whole))
        whole = exchange(whole, axes)
    grad_embed_t = whole.reshape(8, REACH, 8, 128).transpose(0, 2, 1, 3).reshape(HEAD_DIM, BAND)
    far = shift(far, -2)
    (far,) = call(add_body, [(unit, BF16, True)], near(far), near(d1))
    far = shift(far, -2)
    third = ((TOK, 3 * PAIR), BF16, True)
    keep, send = staged_call(final_body, [third] * 2, odd, near(far), near(d0), near(gq))
    got = swap(send)
    grads = staged_call(unpack_body, [((TOK, 2 * PAIR), BF16, False)] * 3, odd, near(keep), near(got))
    return (*grads, grad_embed_t.T)


def solution(mesh):
    fine = jax.sharding.Mesh(mesh.devices.reshape(DIMS), ("y", "zg", "zi", "x", "core"))
    rows = P(SEQ, ("x", "core"))
    return jax.shard_map(
        local,
        mesh=fine,
        in_specs=(rows, rows, rows, rows, P()),
        out_specs=(rows, rows, rows, P()),
        check_vma=False,
    )
```

```python
import jax
import jax.numpy as jnp
from jax import lax
from jax.experimental import pallas as pl
from jax.experimental.pallas import tpu as pltpu
from jax.sharding import PartitionSpec as P


HEAD_DIM = 64
BAND = 512
TOK = 128
REACH = BAND // TOK
HEADS = 2
PAIR = HEADS * HEAD_DIM
ROWS = 2 * TOK
SPAN = BAND + ROWS
DIMS = (4, 4, 4, 4, 2)
SCALE = HEAD_DIM ** (-0.5)
F32 = jnp.float32
BF16 = jnp.bfloat16
NN = ((1,), (0,))
NT = ((1,), (1,))
TN = ((0,), (0,))


def call(body, outs, *args, **kw):
    shapes = [pltpu.VMEM(s, d) if v else jax.ShapeDtypeStruct(s, d) for s, d, v in outs]
    return list(pl.pallas_call(body, out_shape=shapes, **kw)(*args))


def near(x):
    return pltpu.with_memory_space_constraint(x, pltpu.VMEM)


def mm(a, b, dims):
    return lax.dot_general(a, b, (dims, ((), ())), preferred_element_type=F32)


def span(block):
    return slice(block * TOK, (block + 1) * TOK)


def flip_matrix(count):
    row = lax.broadcasted_iota(jnp.int32, (count, count), 0)
    col = lax.broadcasted_iota(jnp.int32, (count, count), 1)
    return jnp.where(row + col == count - 1, 1.0, 0.0).astype(BF16)


def low_lanes(shape):
    return lax.broadcasted_iota(jnp.int32, shape, len(shape) - 1) < HEAD_DIM


def half(b):
    return pl.ds(pl.multiple_of(b * TOK, TOK), TOK)


def pick(take, x):
    low, high = x[:, :PAIR], x[:, PAIR:]
    return jnp.where(take, high, low), jnp.where(take, low, high)


def pack_body(odd, k, v, mine, other):
    for i, x in enumerate((k, v)):
        lanes = slice(i * PAIR, (i + 1) * PAIR)
        mine[:, lanes], other[:, lanes] = pick(odd[0] > 0, x)


def pack_q_body(odd, q, do, emb_t, kv_other, mine, other, erev):
    other[:, : 2 * PAIR] = kv_other[...]
    for i, x in enumerate((q, do)):
        a, b = pick(odd[0] > 0, x)
        mine[:, i * PAIR : (i + 1) * PAIR] = a
        other[:, (i + 2) * PAIR : (i + 3) * PAIR] = b
    flip = flip_matrix(TOK)
    for b in range(REACH):
        back = mm(emb_t[:, span(REACH - 1 - b)], flip, NN).astype(BF16)
        erev[:HEAD_DIM, span(b)] = back
        erev[HEAD_DIM:, span(b)] = back


def unite_body(odd, kv_mine, q_mine, got, near_a, near_b, kv, qs, dos):
    here, there = half(odd[0]), half(1 - odd[0])
    kv[0, here] = near_a[...]
    kv[0, there] = near_b[...]
    kv[1, here] = kv_mine[...]
    kv[1, there] = got[:, : 2 * PAIR]
    low = low_lanes((TOK, PAIR))
    zero = jnp.zeros((TOK, PAIR), BF16)
    for rows, part, first in ((here, q_mine, 0), (there, got, 2)):
        for i, out in enumerate((qs, dos)):
            x = part[:, (first + i) * PAIR : (first + i + 1) * PAIR]
            out[0, rows] = jnp.where(low, x, zero)
            out[1, rows] = jnp.where(low, zero, x)


def main_body(place, qs, dos, erev, kv, far_a, far_b, far, d1, d0, gq, send, gemb, kv2, gqs, d0s):
    here, there = half(place[0]), half(1 - place[0])
    kv2[here] = far_a[...]
    kv2[there] = far_b[...]
    flip = flip_matrix(ROWS)
    row = lax.broadcasted_iota(jnp.int32, (ROWS, SPAN), 0)
    col = lax.broadcasted_iota(jnp.int32, (ROWS, SPAN), 1)
    ahead = col - row - 1
    valid = (ahead >= 0) & (ahead < BAND) & (col >= place[1])
    k = jnp.concatenate([x[:, :PAIR] for x in (kv2, kv.at[0], kv.at[1])], axis=0)
    v = jnp.concatenate([x[:, PAIR:] for x in (kv2, kv.at[0], kv.at[1])], axis=0)
    total = jnp.zeros((PAIR, BAND), F32)
    gk = jnp.zeros((SPAN, PAIR), F32)
    gv = jnp.zeros((SPAN, PAIR), F32)
    gq_parts = []
    for h in range(HEADS):
        q, do = qs[h], dos[h]
        along = jnp.concatenate([mm(q, erev[...], NN), jnp.zeros((ROWS, ROWS), F32)], axis=1)
        s = (pltpu.roll(along, 1, 1, stride=1, stride_axis=0) + mm(q, k, NT)) * SCALE
        s = jnp.where(valid, s, -jnp.inf)
        dp = mm(do, v, NT)
        prob = jnp.exp(s - jnp.max(s, axis=1, keepdims=True))
        prob = prob * (1.0 / jnp.sum(prob, axis=1, keepdims=True))
        prob_b = prob.astype(BF16)
        delta = jnp.sum(prob_b.astype(F32) * dp, axis=1, keepdims=True)
        ds = (prob * (dp - delta) * SCALE).astype(BF16)
        dalong = pltpu.roll(mm(flip, ds, NN), BAND, 1, stride=1, stride_axis=0)[:, :BAND].astype(BF16)
        total = total + mm(mm(flip, q, NN).astype(BF16), dalong, TN)
        gk = gk + mm(ds, q, TN)
        gv = gv + mm(prob_b, do, TN)
        gqe = mm(dalong, erev[...], NT)
        hi = gqe.astype(BF16)
        lo = (gqe - hi.astype(F32)).astype(BF16)
        gq_parts.append(mm(ds, k, NN) + mm(flip, hi, NN) + mm(flip, lo, NN))
    gqs[...] = jnp.where(low_lanes((ROWS, PAIR)), *gq_parts).astype(BF16)
    gq[...] = gqs[here]
    send[:, :PAIR] = gqs[there]
    for part, lanes in ((gk, slice(0, PAIR)), (gv, slice(PAIR, 2 * PAIR))):
        far[:, lanes] = part[:ROWS].astype(BF16)
        d1[:, lanes] = part[ROWS : 2 * ROWS]
        d0s[:, lanes] = part[2 * ROWS :]
    d0[...] = d0s[here]
    send[:, PAIR:] = d0s[there].astype(BF16)
    total = total[:HEAD_DIM] + total[HEAD_DIM:]
    flip = flip_matrix(TOK)
    for b in range(REACH):
        block = total[:, span(REACH - 1 - b)]
        hi = block.astype(BF16)
        lo = (block - hi.astype(F32)).astype(BF16)
        block = mm(hi, flip, NN) + mm(lo, flip, NN)
        for d in range(HEAD_DIM // 8):
            gemb[d * REACH + b] = block[d * 8 : (d + 1) * 8]


def sum_body(x, out):
    out[...] = jnp.broadcast_to(jnp.sum(x[...], axis=0, keepdims=True), out.shape)


def add_body(odd, got, d1, out_a, out_b):
    for rows, out in ((half(odd[0]), out_a), (half(1 - odd[0]), out_b)):
        out[...] = (d1[rows] + got[rows].astype(F32)).astype(BF16)


def final_body(odd, gq, d0, got, got_a, got_b, grad_q, grad_k, grad_v):
    swap = odd[0] > 0
    mine = (d0[...] + got_a[...].astype(F32)).astype(BF16)
    other = (got[:, PAIR:].astype(F32) + got_b[...].astype(F32)).astype(BF16)
    pairs = (gq[...], got[:, :PAIR]), (mine[:, :PAIR], other[:, :PAIR]), (mine[:, PAIR:], other[:, PAIR:])
    for out, (a, b) in zip((grad_q, grad_k, grad_v), pairs):
        out[:, :PAIR] = jnp.where(swap, b, a)
        out[:, PAIR:] = jnp.where(swap, a, b)


SEQ = ("y", "zg", "zi")


def shift(x, steps, cross=False):
    n = lax.axis_size(SEQ)
    pairs = [(s, (s ^ 1 if cross else s) + steps) for s in range(n)]
    return near(lax.ppermute(x, SEQ, [(s, t) for s, t in pairs if 0 <= t < n]))


def exchange(x, axes):
    return lax.all_to_all(x, axes, 0, 0, tiled=True)


def local(query, key_rows, value_matrix_rows, grad_out, rel_embed):
    line, plane = ("zg", "zi"), ("y", "x", "core")
    here = lax.axis_index(SEQ)
    odd = (here & 1).reshape(1)
    sm, vm = pl.BlockSpec(memory_space=pltpu.SMEM), pl.BlockSpec(memory_space=pltpu.VMEM)

    def run(name, body, outs, *args, **kw):
        outs = call(body, outs, *args, in_specs=[sm] + [vm] * (len(args) - 1), **kw)
        return [near(x) for x in outs] if name not in ("main", "final") else outs

    half_unit, unit = ((TOK, 2 * PAIR), BF16, True), (ROWS, 2 * PAIR)
    kv_mine, kv_other = run("pack", pack_body, [half_unit] * 2, odd, key_rows, value_matrix_rows)
    near_a = shift(kv_mine, 2)
    near_b = shift(kv_other, 2, True)
    q_mine, other, erev = run(
        "qpack",
        pack_q_body,
        [half_unit, ((TOK, 4 * PAIR), BF16, True), ((PAIR, BAND), BF16, True)],
        odd, query, grad_out, rel_embed.T, kv_other,
    )
    got = shift(other, 0, True)
    far_a = shift(near_a, 2)
    far_b = shift(near_b, 2)
    heads = ((HEADS, ROWS, PAIR), BF16, True)
    kv, qs, dos = run(
        "unite",
        unite_body,
        [((2, ROWS, 2 * PAIR), BF16, True), heads, heads],
        odd, kv_mine, q_mine, got, near_a, near_b,
    )
    first = ROWS * jnp.maximum(BAND // ROWS - (here >> 1), 0)
    far, d1, d0, gq, send, gemb = run(
        "main",
        main_body,
        [
            (unit, BF16, True),
            (unit, F32, True),
            ((TOK, 2 * PAIR), F32, True),
            ((TOK, PAIR), BF16, True),
            ((TOK, 3 * PAIR), BF16, True),
            ((lax.axis_size(plane), 8, 128), F32, True),
        ],
        jnp.stack([here & 1, first]), qs, dos, erev, kv, far_a, far_b,
        scratch_shapes=[pltpu.VMEM(unit, BF16), pltpu.VMEM((ROWS, PAIR), BF16), pltpu.VMEM(unit, F32)],
    )
    whole = exchange(gemb, plane)
    for axes in (line, plane):
        tiles = ((lax.axis_size(axes), 8, 128), F32, True)
        (whole,) = call(sum_body, [tiles], near(whole))
        whole = exchange(whole, axes)
    grad_embed_t = whole.reshape(8, REACH, 8, 128).transpose(0, 2, 1, 3).reshape(HEAD_DIM, BAND)
    back = shift(far, -2)
    swapped = shift(send, 0, True)
    out_a, out_b = run("add", add_body, [half_unit] * 2, odd, back, near(d1))
    out_a = shift(out_a, -2)
    out_b = shift(out_b, -2, True)
    grads = run("final", final_body, [((TOK, 2 * PAIR), BF16, False)] * 3, odd, near(gq), near(d0), swapped, out_a, out_b)
    return (*grads, grad_embed_t.T)


def solution(mesh):
    fine = jax.sharding.Mesh(mesh.devices.reshape(DIMS), ("y", "zg", "zi", "x", "core"))
    rows = P(SEQ, ("x", "core"))
    return jax.shard_map(
        local,
        mesh=fine,
        in_specs=(rows, rows, rows, rows, P()),
        out_specs=(rows, rows, rows, P()),
        check_vma=False,
    )
```

```python
import jax
import jax.numpy as jnp
from jax import lax
from jax.experimental import pallas as pl
from jax.experimental.pallas import tpu as pltpu
from jax.sharding import PartitionSpec as P


HEAD_DIM = 64
BAND = 512
TOK = 128
REACH = BAND // TOK
HEADS = 2
PAIR = HEADS * HEAD_DIM
ROWS = 2 * TOK
SPAN = BAND + ROWS
DIMS = (4, 4, 4, 4, 2)
SCALE = HEAD_DIM ** (-0.5)
F32 = jnp.float32
BF16 = jnp.bfloat16
NN = ((1,), (0,))
NT = ((1,), (1,))
TN = ((0,), (0,))


def call(body, outs, *args, **kw):
    shapes = [pltpu.VMEM(s, d) if v else jax.ShapeDtypeStruct(s, d) for s, d, v in outs]
    return list(pl.pallas_call(body, out_shape=shapes, **kw)(*args))


def near(x):
    return pltpu.with_memory_space_constraint(x, pltpu.VMEM)


def mm(a, b, dims):
    return lax.dot_general(a, b, (dims, ((), ())), preferred_element_type=F32)


def span(block):
    return slice(block * TOK, (block + 1) * TOK)


def flip_matrix(count):
    row = lax.broadcasted_iota(jnp.int32, (count, count), 0)
    col = lax.broadcasted_iota(jnp.int32, (count, count), 1)
    return jnp.where(row + col == count - 1, 1.0, 0.0).astype(BF16)


def low_lanes(shape):
    return lax.broadcasted_iota(jnp.int32, shape, len(shape) - 1) < HEAD_DIM


def half(b):
    return pl.ds(pl.multiple_of(b * TOK, TOK), TOK)


def pick(take, x):
    low, high = x[:, :PAIR], x[:, PAIR:]
    return jnp.where(take, high, low), jnp.where(take, low, high)


def pack_body(odd, k, v, q, do, emb_t, kv_mine, kv_other, q_mine, other, erev):
    for i, x in enumerate((k, v, q, do)):
        a, b = pick(odd[0] > 0, x)
        other[:, i * PAIR : (i + 1) * PAIR] = b
        lanes = slice(i % 2 * PAIR, (i % 2 + 1) * PAIR)
        (kv_mine if i < 2 else q_mine)[:, lanes] = a
        if i < 2:
            kv_other[:, lanes] = b
    flip = flip_matrix(TOK)
    for b in range(REACH):
        back = mm(emb_t[:, span(REACH - 1 - b)], flip, NN).astype(BF16)
        erev[:HEAD_DIM, span(b)] = back
        erev[HEAD_DIM:, span(b)] = back


def early_body(odd, kv_mine, q_mine, got, near_a, near_b, kv, qs, dos):
    here, there = half(odd[0]), half(1 - odd[0])
    kv[0, here] = near_a[...]
    kv[0, there] = near_b[...]
    kv[1, here] = kv_mine[...]
    kv[1, there] = got[:, : 2 * PAIR]
    low = low_lanes((TOK, PAIR))
    zero = jnp.zeros((TOK, PAIR), BF16)
    for rows, part, first in ((here, q_mine, 0), (there, got, 2)):
        for i, out in enumerate((qs, dos)):
            x = part[:, (first + i) * PAIR : (first + i + 1) * PAIR]
            out[0, rows] = jnp.where(low, x, zero)
            out[1, rows] = jnp.where(low, zero, x)


def main_body(odd, first, qs, dos, erev, kv, far_a, far_b, far, d1, d0, gq, gemb, kv2):
    here, there = half(odd[0]), half(1 - odd[0])
    kv2[here] = far_a[...]
    kv2[there] = far_b[...]
    flip = flip_matrix(ROWS)
    row = lax.broadcasted_iota(jnp.int32, (ROWS, SPAN), 0)
    col = lax.broadcasted_iota(jnp.int32, (ROWS, SPAN), 1)
    ahead = col - row - 1
    valid = (ahead >= 0) & (ahead < BAND) & (col >= first[0])
    k = jnp.concatenate([x[:, :PAIR] for x in (kv2, kv.at[0], kv.at[1])], axis=0)
    v = jnp.concatenate([x[:, PAIR:] for x in (kv2, kv.at[0], kv.at[1])], axis=0)
    total = jnp.zeros((PAIR, BAND), F32)
    gk = jnp.zeros((SPAN, PAIR), F32)
    gv = jnp.zeros((SPAN, PAIR), F32)
    gq_parts = []
    for h in range(HEADS):
        q, do = qs[h], dos[h]
        along = jnp.concatenate([mm(q, erev[...], NN), jnp.zeros((ROWS, ROWS), F32)], axis=1)
        s = (pltpu.roll(along, 1, 1, stride=1, stride_axis=0) + mm(q, k, NT)) * SCALE
        s = jnp.where(valid, s, -jnp.inf)
        dp = mm(do, v, NT)
        prob = jnp.exp(s - jnp.max(s, axis=1, keepdims=True))
        prob = prob * (1.0 / jnp.sum(prob, axis=1, keepdims=True))
        prob_b = prob.astype(BF16)
        delta = jnp.sum(prob_b.astype(F32) * dp, axis=1, keepdims=True)
        ds = (prob * (dp - delta) * SCALE).astype(BF16)
        dalong = pltpu.roll(mm(flip, ds, NN), BAND, 1, stride=1, stride_axis=0)[:, :BAND].astype(BF16)
        total = total + mm(mm(flip, q, NN).astype(BF16), dalong, TN)
        gk = gk + mm(ds, q, TN)
        gv = gv + mm(prob_b, do, TN)
        gqe = mm(dalong, erev[...], NT)
        hi = gqe.astype(BF16)
        lo = (gqe - hi.astype(F32)).astype(BF16)
        gq_parts.append(mm(ds, k, NN) + mm(flip, hi, NN) + mm(flip, lo, NN))
    gq[...] = jnp.where(low_lanes((ROWS, PAIR)), *gq_parts).astype(BF16)
    for part, lanes in ((gk, slice(0, PAIR)), (gv, slice(PAIR, 2 * PAIR))):
        far[:, lanes] = part[:ROWS].astype(BF16)
        d1[:, lanes] = part[ROWS : 2 * ROWS]
        d0[:, lanes] = part[2 * ROWS :]
    total = total[:HEAD_DIM] + total[HEAD_DIM:]
    flip = flip_matrix(TOK)
    for b in range(REACH):
        block = total[:, span(REACH - 1 - b)]
        hi = block.astype(BF16)
        lo = (block - hi.astype(F32)).astype(BF16)
        block = mm(hi, flip, NN) + mm(lo, flip, NN)
        for d in range(HEAD_DIM // 8):
            gemb[d * REACH + b] = block[d * 8 : (d + 1) * 8]


def sum_body(x, out):
    out[...] = jnp.broadcast_to(jnp.sum(x[...], axis=0, keepdims=True), out.shape)


def add_body(got, d1, out):
    out[...] = (d1[...] + got[...].astype(F32)).astype(BF16)


def final_body(odd, got, d0, gq, keep, send):
    for rows, out in ((half(odd[0]), keep), (half(1 - odd[0]), send)):
        out[:, :PAIR] = gq[rows]
        out[:, PAIR:] = (d0[rows] + got[rows].astype(F32)).astype(BF16)


def unpack_body(odd, keep, got, *outs):
    swap = odd[0] > 0
    for i, out in enumerate(outs):
        lanes = slice(i * PAIR, (i + 1) * PAIR)
        a, b = keep[:, lanes], got[:, lanes]
        out[:, :PAIR] = jnp.where(swap, b, a)
        out[:, PAIR:] = jnp.where(swap, a, b)


SEQ = ("y", "zg", "zi")


def shift(x, steps, cross=False):
    n = lax.axis_size(SEQ)
    pairs = [(s, (s ^ 1 if cross else s) + steps) for s in range(n)]
    return near(lax.ppermute(x, SEQ, [(s, t) for s, t in pairs if 0 <= t < n]))


def exchange(x, axes):
    return lax.all_to_all(x, axes, 0, 0, tiled=True)


def local(query, key_rows, value_matrix_rows, grad_out, rel_embed):
    line, plane = ("zg", "zi"), ("y", "x", "core")
    here = lax.axis_index(SEQ)
    odd = (here & 1).reshape(1)
    first = (ROWS * jnp.maximum(BAND // ROWS - (here >> 1), 0)).reshape(1)
    sm, vm = pl.BlockSpec(memory_space=pltpu.SMEM), pl.BlockSpec(memory_space=pltpu.VMEM)

    def run(name, body, outs, scalars, *args, **kw):
        specs = [sm] * len(scalars) + [vm] * len(args)
        outs = call(body, outs, *scalars, *args, in_specs=specs, **kw)
        return [near(x) for x in outs] if name != "unpack" else outs

    half_unit, unit = ((TOK, 2 * PAIR), BF16, True), (ROWS, 2 * PAIR)
    kv_mine, kv_other, q_mine, other, erev = run(
        "pack",
        pack_body,
        [half_unit] * 3 + [((TOK, 4 * PAIR), BF16, True), ((PAIR, BAND), BF16, True)],
        [odd], key_rows, value_matrix_rows, query, grad_out, rel_embed.T,
    )
    got = shift(other, 0, True)
    near_a = shift(kv_mine, 2)
    near_b = shift(kv_other, 2, True)
    far_a = shift(near_a, 2)
    far_b = shift(near_b, 2)
    heads = ((HEADS, ROWS, PAIR), BF16, True)
    kv, qs, dos = run(
        "early",
        early_body,
        [((2, ROWS, 2 * PAIR), BF16, True), heads, heads],
        [odd], kv_mine, q_mine, got, near_a, near_b,
    )
    far, d1, d0, gq, gemb = run(
        "main",
        main_body,
        [(unit, BF16, True), (unit, F32, True), (unit, F32, True), ((ROWS, PAIR), BF16, True)]
        + [((lax.axis_size(plane), 8, 128), F32, True)],
        [odd, first], qs, dos, erev, kv, far_a, far_b,
        scratch_shapes=[pltpu.VMEM(unit, BF16)],
    )
    whole = exchange(gemb, plane)
    for axes in (line, plane):
        tiles = ((lax.axis_size(axes), 8, 128), F32, True)
        (whole,) = call(sum_body, [tiles], near(whole))
        whole = exchange(whole, axes)
    grad_embed_t = whole.reshape(8, REACH, 8, 128).transpose(0, 2, 1, 3).reshape(HEAD_DIM, BAND)
    back = shift(far, -2)
    (back,) = run("add", add_body, [(unit, BF16, True)], [], back, d1)
    back = shift(back, -2)
    third = ((TOK, 3 * PAIR), BF16, True)
    keep, send = run("final", final_body, [third] * 2, [odd], back, d0, gq)
    got = shift(send, 0, True)
    grads = run("unpack", unpack_body, [((TOK, 2 * PAIR), BF16, False)] * 3, [odd], keep, got)
    return (*grads, grad_embed_t.T)


def solution(mesh):
    fine = jax.sharding.Mesh(mesh.devices.reshape(DIMS), ("y", "zg", "zi", "x", "core"))
    rows = P(SEQ, ("x", "core"))
    return jax.shard_map(
        local,
        mesh=fine,
        in_specs=(rows, rows, rows, rows, P()),
        out_specs=(rows, rows, rows, P()),
        check_vma=False,
    )
```

```python
import jax
import jax.numpy as jnp
from jax import lax
from jax.experimental import pallas as pl
from jax.experimental.pallas import tpu as pltpu
from jax.sharding import PartitionSpec as P


HEAD_DIM = 64
BAND = 512
TOK = 128
REACH = BAND // TOK
HEADS = 2
PAIR = HEADS * HEAD_DIM
ROWS = 2 * TOK
SPAN = BAND + ROWS
DIMS = (4, 4, 4, 4, 2)
SCALE = HEAD_DIM ** (-0.5)
F32 = jnp.float32
BF16 = jnp.bfloat16
NN = ((1,), (0,))
NT = ((1,), (1,))
TN = ((0,), (0,))


def call(body, outs, *args, **kw):
    shapes = [pltpu.VMEM(s, d) if v else jax.ShapeDtypeStruct(s, d) for s, d, v in outs]
    return list(pl.pallas_call(body, out_shape=shapes, **kw)(*args))


def near(x):
    return pltpu.with_memory_space_constraint(x, pltpu.VMEM)


def mm(a, b, dims):
    return lax.dot_general(a, b, (dims, ((), ())), preferred_element_type=F32)


def span(block):
    return slice(block * TOK, (block + 1) * TOK)


def flip_matrix(count):
    row = lax.broadcasted_iota(jnp.int32, (count, count), 0)
    col = lax.broadcasted_iota(jnp.int32, (count, count), 1)
    return jnp.where(row + col == count - 1, 1.0, 0.0).astype(BF16)


def low_lanes(shape):
    return lax.broadcasted_iota(jnp.int32, shape, len(shape) - 1) < HEAD_DIM


def half(b):
    return pl.ds(pl.multiple_of(b * TOK, TOK), TOK)


def pick(take, x):
    low, high = x[:, :PAIR], x[:, PAIR:]
    return jnp.where(take, high, low), jnp.where(take, low, high)


def pack_body(odd, k, v, q, do, emb_t, kv_mine, kv_other, q_mine, other, erev):
    for i, x in enumerate((k, v, q, do)):
        a, b = pick(odd[0] > 0, x)
        other[:, i * PAIR : (i + 1) * PAIR] = b
        lanes = slice(i % 2 * PAIR, (i % 2 + 1) * PAIR)
        (kv_mine if i < 2 else q_mine)[:, lanes] = a
        if i < 2:
            kv_other[:, lanes] = b
    flip = flip_matrix(TOK)
    for b in range(REACH):
        back = mm(emb_t[:, span(REACH - 1 - b)], flip, NN).astype(BF16)
        erev[:HEAD_DIM, span(b)] = back
        erev[HEAD_DIM:, span(b)] = back


def early_body(odd, kv_mine, q_mine, got, near_a, near_b, kv, qs, dos, qf):
    here, there = half(odd[0]), half(1 - odd[0])
    kv[0, here] = near_a[...]
    kv[0, there] = near_b[...]
    kv[1, here] = kv_mine[...]
    kv[1, there] = got[:, : 2 * PAIR]
    low = low_lanes((TOK, PAIR))
    zero = jnp.zeros((TOK, PAIR), BF16)
    for rows, part, first in ((here, q_mine, 0), (there, got, 2)):
        for i, out in enumerate((qs, dos)):
            x = part[:, (first + i) * PAIR : (first + i + 1) * PAIR]
            out[0, rows] = jnp.where(low, x, zero)
            out[1, rows] = jnp.where(low, zero, x)
    flip = flip_matrix(ROWS)
    for h in range(HEADS):
        qf[h] = mm(flip, qs[h], NN).astype(BF16)


def main_body(odd, first, qs, dos, qf, erev, kv, far_a, far_b, far, d1, d0, gq, gemb, kv2):
    here, there = half(odd[0]), half(1 - odd[0])
    kv2[here] = far_a[...]
    kv2[there] = far_b[...]
    flip = flip_matrix(ROWS)
    row = lax.broadcasted_iota(jnp.int32, (ROWS, SPAN), 0)
    col = lax.broadcasted_iota(jnp.int32, (ROWS, SPAN), 1)
    ahead = col - row - 1
    valid = (ahead >= 0) & (ahead < BAND) & (col >= first[0])
    k = jnp.concatenate([x[:, :PAIR] for x in (kv2, kv.at[0], kv.at[1])], axis=0)
    v = jnp.concatenate([x[:, PAIR:] for x in (kv2, kv.at[0], kv.at[1])], axis=0)
    total = jnp.zeros((PAIR, BAND), F32)
    gk = jnp.zeros((PAIR, SPAN), F32)
    gv = jnp.zeros((PAIR, SPAN), F32)
    gq_parts, gqe_parts = [], []
    for h in range(HEADS):
        q, do = qs[h], dos[h]
        along = jnp.concatenate([mm(q, erev[...], NN), jnp.zeros((ROWS, ROWS), F32)], axis=1)
        s = (pltpu.roll(along, 1, 1, stride=1, stride_axis=0) + mm(q, k, NT)) * SCALE
        s = jnp.where(valid, s, -jnp.inf)
        dp = mm(do, v, NT)
        prob = jnp.exp(s - jnp.max(s, axis=1, keepdims=True))
        prob = prob * (1.0 / jnp.sum(prob, axis=1, keepdims=True))
        prob_b = prob.astype(BF16)
        delta = jnp.sum(prob_b.astype(F32) * dp, axis=1, keepdims=True)
        ds = (prob * (dp - delta) * SCALE).astype(BF16)
        dalong = pltpu.roll(mm(flip, ds, NN), BAND, 1, stride=1, stride_axis=0)[:, :BAND].astype(BF16)
        total = total + mm(qf[h], dalong, TN)
        gk = gk + mm(q, ds, TN)
        gv = gv + mm(do, prob_b, TN)
        gq_parts.append(mm(ds, k, NN))
        gqe_parts.append(mm(dalong, erev[...], NT))
    low = low_lanes((ROWS, PAIR))
    gqe = jnp.where(low, *gqe_parts)
    hi = gqe.astype(BF16)
    lo = (gqe - hi.astype(F32)).astype(BF16)
    gq[...] = (jnp.where(low, *gq_parts) + mm(flip, hi, NN) + mm(flip, lo, NN)).astype(BF16)
    for part, lanes in ((gk.T, slice(0, PAIR)), (gv.T, slice(PAIR, 2 * PAIR))):
        far[:, lanes] = part[:ROWS].astype(BF16)
        d1[:, lanes] = part[ROWS : 2 * ROWS]
        d0[:, lanes] = part[2 * ROWS :]
    total = total[:HEAD_DIM] + total[HEAD_DIM:]
    flip = flip_matrix(TOK)
    for b in range(REACH):
        block = total[:, span(REACH - 1 - b)]
        hi = block.astype(BF16)
        lo = (block - hi.astype(F32)).astype(BF16)
        block = mm(hi, flip, NN) + mm(lo, flip, NN)
        for d in range(HEAD_DIM // 8):
            gemb[d * REACH + b] = block[d * 8 : (d + 1) * 8]


def sum_body(x, out):
    out[...] = jnp.broadcast_to(jnp.sum(x[...], axis=0, keepdims=True), out.shape)


def add_body(got, d1, out):
    out[...] = (d1[...] + got[...].astype(F32)).astype(BF16)


def final_body(odd, got, d0, gq, keep, send):
    for rows, out in ((half(odd[0]), keep), (half(1 - odd[0]), send)):
        out[:, :PAIR] = gq[rows]
        out[:, PAIR:] = (d0[rows] + got[rows].astype(F32)).astype(BF16)


def unpack_body(odd, keep, got, *outs):
    swap = odd[0] > 0
    for i, out in enumerate(outs):
        lanes = slice(i * PAIR, (i + 1) * PAIR)
        a, b = keep[:, lanes], got[:, lanes]
        out[:, :PAIR] = jnp.where(swap, b, a)
        out[:, PAIR:] = jnp.where(swap, a, b)


SEQ = ("y", "zg", "zi")


def shift(x, steps, cross=False):
    n = lax.axis_size(SEQ)
    pairs = [(s, (s ^ 1 if cross else s) + steps) for s in range(n)]
    return near(lax.ppermute(x, SEQ, [(s, t) for s, t in pairs if 0 <= t < n]))


def exchange(x, axes):
    return lax.all_to_all(x, axes, 0, 0, tiled=True)


def local(query, key_rows, value_matrix_rows, grad_out, rel_embed):
    line, plane = ("zg", "zi"), ("y", "x", "core")
    here = lax.axis_index(SEQ)
    odd = (here & 1).reshape(1)
    first = (ROWS * jnp.maximum(BAND // ROWS - (here >> 1), 0)).reshape(1)
    sm, vm = pl.BlockSpec(memory_space=pltpu.SMEM), pl.BlockSpec(memory_space=pltpu.VMEM)

    def run(name, body, outs, scalars, *args, **kw):
        specs = [sm] * len(scalars) + [vm] * len(args)
        outs = call(body, outs, *scalars, *args, in_specs=specs, **kw)
        return [near(x) for x in outs] if name != "unpack" else outs

    half_unit, unit = ((TOK, 2 * PAIR), BF16, True), (ROWS, 2 * PAIR)
    kv_mine, kv_other, q_mine, other, erev = run(
        "pack",
        pack_body,
        [half_unit] * 3 + [((TOK, 4 * PAIR), BF16, True), ((PAIR, BAND), BF16, True)],
        [odd], key_rows, value_matrix_rows, query, grad_out, rel_embed.T,
    )
    got = shift(other, 0, True)
    near_a = shift(kv_mine, 2)
    near_b = shift(kv_other, 2, True)
    far_a = shift(near_a, 2)
    far_b = shift(near_b, 2)
    heads = ((HEADS, ROWS, PAIR), BF16, True)
    kv, qs, dos, qf = run(
        "early",
        early_body,
        [((2, ROWS, 2 * PAIR), BF16, True), heads, heads, heads],
        [odd], kv_mine, q_mine, got, near_a, near_b,
    )
    far, d1, d0, gq, gemb = run(
        "main",
        main_body,
        [(unit, BF16, True), (unit, F32, True), (unit, F32, True), ((ROWS, PAIR), BF16, True)]
        + [((lax.axis_size(plane), 8, 128), F32, True)],
        [odd, first], qs, dos, qf, erev, kv, far_a, far_b,
        scratch_shapes=[pltpu.VMEM(unit, BF16)],
    )
    whole = exchange(gemb, plane)
    for axes in (line, plane):
        tiles = ((lax.axis_size(axes), 8, 128), F32, True)
        (whole,) = call(sum_body, [tiles], near(whole))
        whole = exchange(whole, axes)
    grad_embed_t = whole.reshape(8, REACH, 8, 128).transpose(0, 2, 1, 3).reshape(HEAD_DIM, BAND)
    back = shift(far, -2)
    (back,) = run("add", add_body, [(unit, BF16, True)], [], back, d1)
    back = shift(back, -2)
    third = ((TOK, 3 * PAIR), BF16, True)
    keep, send = run("final", final_body, [third] * 2, [odd], back, d0, gq)
    got = shift(send, 0, True)
    grads = run("unpack", unpack_body, [((TOK, 2 * PAIR), BF16, False)] * 3, [odd], keep, got)
    return (*grads, grad_embed_t.T)


def solution(mesh):
    fine = jax.sharding.Mesh(mesh.devices.reshape(DIMS), ("y", "zg", "zi", "x", "core"))
    rows = P(SEQ, ("x", "core"))
    return jax.shard_map(
        local,
        mesh=fine,
        in_specs=(rows, rows, rows, rows, P()),
        out_specs=(rows, rows, rows, P()),
        check_vma=False,
    )
```

```python
import jax
import jax.numpy as jnp
from jax import lax
from jax.experimental import pallas as pl
from jax.experimental.pallas import tpu as pltpu
from jax.sharding import PartitionSpec as P


HEAD_DIM = 64
BAND = 512
TOK = 128
REACH = BAND // TOK
HEADS = 2
PAIR = HEADS * HEAD_DIM
ROWS = 2 * TOK
SPAN = BAND + ROWS
DIMS = (4, 4, 4, 4, 2)
SCALE = HEAD_DIM ** (-0.5)
F32 = jnp.float32
BF16 = jnp.bfloat16
NN = ((1,), (0,))
NT = ((1,), (1,))
TN = ((0,), (0,))


def call(body, outs, *args, **kw):
    shapes = [pltpu.VMEM(s, d) if v else jax.ShapeDtypeStruct(s, d) for s, d, v in outs]
    return list(pl.pallas_call(body, out_shape=shapes, **kw)(*args))


def near(x):
    return pltpu.with_memory_space_constraint(x, pltpu.VMEM)


def mm(a, b, dims):
    return lax.dot_general(a, b, (dims, ((), ())), preferred_element_type=F32)


def span(block):
    return slice(block * TOK, (block + 1) * TOK)


def flip_matrix(count):
    row = lax.broadcasted_iota(jnp.int32, (count, count), 0)
    col = lax.broadcasted_iota(jnp.int32, (count, count), 1)
    return jnp.where(row + col == count - 1, 1.0, 0.0).astype(BF16)


def low_lanes(shape):
    return lax.broadcasted_iota(jnp.int32, shape, len(shape) - 1) < HEAD_DIM


def half(b):
    return pl.ds(pl.multiple_of(b * TOK, TOK), TOK)


def pick(take, x):
    low, high = x[:, :PAIR], x[:, PAIR:]
    return jnp.where(take, high, low), jnp.where(take, low, high)


def pack_body(odd, k, v, q, do, kv_mine, kv_other, q_mine, other):
    for i, x in enumerate((k, v, q, do)):
        a, b = pick(odd[0] > 0, x)
        other[:, i * PAIR : (i + 1) * PAIR] = b
        lanes = slice(i % 2 * PAIR, (i % 2 + 1) * PAIR)
        (kv_mine if i < 2 else q_mine)[:, lanes] = a
        if i < 2:
            kv_other[:, lanes] = b


def early_body(odd, kv_mine, q_mine, got, near_a, near_b, emb_t, erev, kv, qs, dos, qf):
    here, there = half(odd[0]), half(1 - odd[0])
    kv[0, here] = near_a[...]
    kv[0, there] = near_b[...]
    kv[1, here] = kv_mine[...]
    kv[1, there] = got[:, : 2 * PAIR]
    low = low_lanes((TOK, PAIR))
    zero = jnp.zeros((TOK, PAIR), BF16)
    for rows, part, first in ((here, q_mine, 0), (there, got, 2)):
        for i, out in enumerate((qs, dos)):
            x = part[:, (first + i) * PAIR : (first + i + 1) * PAIR]
            out[0, rows] = jnp.where(low, x, zero)
            out[1, rows] = jnp.where(low, zero, x)
    flip = flip_matrix(TOK)
    for b in range(REACH):
        back = mm(emb_t[:, span(REACH - 1 - b)], flip, NN).astype(BF16)
        erev[:HEAD_DIM, span(b)] = back
        erev[HEAD_DIM:, span(b)] = back
    flip = flip_matrix(ROWS)
    for h in range(HEADS):
        qf[h] = mm(flip, qs[h], NN).astype(BF16)


def main_body(odd, first, qs, dos, qf, erev, kv, far_a, far_b, far, d1, d0, gq, gemb, kv2):
    here, there = half(odd[0]), half(1 - odd[0])
    kv2[here] = far_a[...]
    kv2[there] = far_b[...]
    flip = flip_matrix(ROWS)
    row = lax.broadcasted_iota(jnp.int32, (ROWS, SPAN), 0)
    col = lax.broadcasted_iota(jnp.int32, (ROWS, SPAN), 1)
    ahead = col - row - 1
    valid = (ahead >= 0) & (ahead < BAND) & (col >= first[0])
    k = jnp.concatenate([x[:, :PAIR] for x in (kv2, kv.at[0], kv.at[1])], axis=0)
    v = jnp.concatenate([x[:, PAIR:] for x in (kv2, kv.at[0], kv.at[1])], axis=0)
    total = jnp.zeros((PAIR, BAND), F32)
    gk = jnp.zeros((PAIR, SPAN), F32)
    gv = jnp.zeros((PAIR, SPAN), F32)
    gq_parts, gqe_parts = [], []
    for h in range(HEADS):
        q, do = qs[h], dos[h]
        along = jnp.concatenate([mm(q, erev[...], NN), jnp.zeros((ROWS, ROWS), F32)], axis=1)
        s = (pltpu.roll(along, 1, 1, stride=1, stride_axis=0) + mm(q, k, NT)) * SCALE
        s = jnp.where(valid, s, -jnp.inf)
        dp = mm(do, v, NT)
        prob = jnp.exp(s - jnp.max(s, axis=1, keepdims=True))
        prob = prob * (1.0 / jnp.sum(prob, axis=1, keepdims=True))
        prob_b = prob.astype(BF16)
        delta = jnp.sum(prob_b.astype(F32) * dp, axis=1, keepdims=True)
        ds = (prob * (dp - delta) * SCALE).astype(BF16)
        dalong = pltpu.roll(mm(flip, ds, NN), BAND, 1, stride=1, stride_axis=0)[:, :BAND].astype(BF16)
        total = total + mm(qf[h], dalong, TN)
        gk = gk + mm(q, ds, TN)
        gv = gv + mm(do, prob_b, TN)
        gq_parts.append(mm(ds, k, NN))
        gqe_parts.append(mm(dalong, erev[...], NT))
    low = low_lanes((ROWS, PAIR))
    gqe = jnp.where(low, *gqe_parts)
    hi = gqe.astype(BF16)
    lo = (gqe - hi.astype(F32)).astype(BF16)
    gq[...] = (jnp.where(low, *gq_parts) + mm(flip, hi, NN) + mm(flip, lo, NN)).astype(BF16)
    for part, lanes in ((gk.T, slice(0, PAIR)), (gv.T, slice(PAIR, 2 * PAIR))):
        far[:, lanes] = part[:ROWS].astype(BF16)
        d1[:, lanes] = part[ROWS : 2 * ROWS]
        d0[:, lanes] = part[2 * ROWS :]
    total = total[:HEAD_DIM] + total[HEAD_DIM:]
    flip = flip_matrix(TOK)
    for b in range(REACH):
        block = total[:, span(REACH - 1 - b)]
        hi = block.astype(BF16)
        lo = (block - hi.astype(F32)).astype(BF16)
        block = mm(hi, flip, NN) + mm(lo, flip, NN)
        for d in range(HEAD_DIM // 8):
            gemb[d * REACH + b] = block[d * 8 : (d + 1) * 8].astype(BF16)


def sum_body(x, out):
    total = jnp.sum(x[...].astype(F32), axis=0, keepdims=True)
    out[...] = jnp.broadcast_to(total, out.shape).astype(BF16)


def add_body(got, d1, out):
    out[...] = (d1[...] + got[...].astype(F32)).astype(BF16)


def final_body(odd, got, d0, gq, keep, send):
    for rows, out in ((half(odd[0]), keep), (half(1 - odd[0]), send)):
        out[:, :PAIR] = gq[rows]
        out[:, PAIR:] = (d0[rows] + got[rows].astype(F32)).astype(BF16)


def unpack_body(odd, keep, got, *outs):
    swap = odd[0] > 0
    for i, out in enumerate(outs):
        lanes = slice(i * PAIR, (i + 1) * PAIR)
        a, b = keep[:, lanes], got[:, lanes]
        out[:, :PAIR] = jnp.where(swap, b, a)
        out[:, PAIR:] = jnp.where(swap, a, b)


SEQ = ("y", "zg", "zi")


def shift(x, steps, cross=False):
    n = lax.axis_size(SEQ)
    pairs = [(s, (s ^ 1 if cross else s) + steps) for s in range(n)]
    return near(lax.ppermute(x, SEQ, [(s, t) for s, t in pairs if 0 <= t < n]))


def exchange(x, axes):
    return lax.all_to_all(x, axes, 0, 0, tiled=True)


def local(query, key_rows, value_matrix_rows, grad_out, rel_embed):
    line, plane = ("zg", "zi"), ("y", "x", "core")
    here = lax.axis_index(SEQ)
    odd = (here & 1).reshape(1)
    first = (ROWS * jnp.maximum(BAND // ROWS - (here >> 1), 0)).reshape(1)
    sm, vm = pl.BlockSpec(memory_space=pltpu.SMEM), pl.BlockSpec(memory_space=pltpu.VMEM)

    def run(name, body, outs, scalars, *args, **kw):
        specs = [sm] * len(scalars) + [vm] * len(args)
        outs = call(body, outs, *scalars, *args, in_specs=specs, **kw)
        return [near(x) for x in outs] if name != "unpack" else outs

    half_unit, unit = ((TOK, 2 * PAIR), BF16, True), (ROWS, 2 * PAIR)
    kv_mine, kv_other, q_mine, other = run(
        "pack",
        pack_body,
        [half_unit] * 3 + [((TOK, 4 * PAIR), BF16, True)],
        [odd], key_rows, value_matrix_rows, query, grad_out,
    )
    got = shift(other, 0, True)
    near_a = shift(kv_mine, 2)
    near_b = shift(kv_other, 2, True)
    far_a = shift(near_a, 2)
    far_b = shift(near_b, 2)
    heads = ((HEADS, ROWS, PAIR), BF16, True)
    erev, kv, qs, dos, qf = run(
        "early",
        early_body,
        [((PAIR, BAND), BF16, True), ((2, ROWS, 2 * PAIR), BF16, True), heads, heads, heads],
        [odd], kv_mine, q_mine, got, near_a, near_b, rel_embed.T,
    )
    far, d1, d0, gq, gemb = run(
        "main",
        main_body,
        [(unit, BF16, True), (unit, F32, True), (unit, F32, True), ((ROWS, PAIR), BF16, True)]
        + [((lax.axis_size(plane), 8, 128), BF16, True)],
        [odd, first], qs, dos, qf, erev, kv, far_a, far_b,
        scratch_shapes=[pltpu.VMEM(unit, BF16)],
    )
    whole = exchange(gemb, plane)
    for axes in (line, plane):
        tiles = ((lax.axis_size(axes), 8, 128), BF16, True)
        (whole,) = call(sum_body, [tiles], near(whole))
        whole = exchange(whole, axes)
    grad_embed_t = whole.astype(F32).reshape(8, REACH, 8, 128).transpose(0, 2, 1, 3).reshape(HEAD_DIM, BAND)
    back = shift(far, -2)
    (back,) = run("add", add_body, [(unit, BF16, True)], [], back, d1)
    back = shift(back, -2)
    third = ((TOK, 3 * PAIR), BF16, True)
    keep, send = run("final", final_body, [third] * 2, [odd], back, d0, gq)
    got = shift(send, 0, True)
    grads = run("unpack", unpack_body, [((TOK, 2 * PAIR), BF16, False)] * 3, [odd], keep, got)
    return (*grads, grad_embed_t.T)


def solution(mesh):
    fine = jax.sharding.Mesh(mesh.devices.reshape(DIMS), ("y", "zg", "zi", "x", "core"))
    rows = P(SEQ, ("x", "core"))
    return jax.shard_map(
        local,
        mesh=fine,
        in_specs=(rows, rows, rows, rows, P()),
        out_specs=(rows, rows, rows, P()),
        check_vma=False,
    )
```

```python
import jax
import jax.numpy as jnp
from jax import lax
from jax.experimental import pallas as pl
from jax.experimental.pallas import tpu as pltpu
from jax.sharding import PartitionSpec as P


HEAD_DIM = 64
BAND = 512
TOK = 128
REACH = BAND // TOK
HEADS = 2
PAIR = HEADS * HEAD_DIM
ROWS = 2 * TOK
SPAN = BAND + ROWS
DIMS = (4, 4, 4, 4, 2)
SCALE = HEAD_DIM ** (-0.5)
F32 = jnp.float32
BF16 = jnp.bfloat16
NN = ((1,), (0,))
NT = ((1,), (1,))
TN = ((0,), (0,))


def call(body, outs, *args, **kw):
    shapes = [pltpu.VMEM(s, d) if v else jax.ShapeDtypeStruct(s, d) for s, d, v in outs]
    return list(pl.pallas_call(body, out_shape=shapes, **kw)(*args))


def near(x):
    return pltpu.with_memory_space_constraint(x, pltpu.VMEM)


def mm(a, b, dims):
    return lax.dot_general(a, b, (dims, ((), ())), preferred_element_type=F32)


def span(block):
    return slice(block * TOK, (block + 1) * TOK)


def flip_matrix(count):
    row = lax.broadcasted_iota(jnp.int32, (count, count), 0)
    col = lax.broadcasted_iota(jnp.int32, (count, count), 1)
    return jnp.where(row + col == count - 1, 1.0, 0.0).astype(BF16)


def low_lanes(shape):
    return lax.broadcasted_iota(jnp.int32, shape, len(shape) - 1) < HEAD_DIM


def half(b):
    return pl.ds(pl.multiple_of(b * TOK, TOK), TOK)


def pick(take, x):
    low, high = x[:, :PAIR], x[:, PAIR:]
    return jnp.where(take, high, low), jnp.where(take, low, high)


def pack_body(odd, k, v, q, do, kv_mine, kv_other, q_mine, other):
    for i, x in enumerate((k, v, q, do)):
        a, b = pick(odd[0] > 0, x)
        other[:, i * PAIR : (i + 1) * PAIR] = b
        lanes = slice(i % 2 * PAIR, (i % 2 + 1) * PAIR)
        (kv_mine if i < 2 else q_mine)[:, lanes] = a
        if i < 2:
            kv_other[:, lanes] = b


def early_body(odd, kv_mine, q_mine, got, near_a, near_b, emb_t, erev, kv, qs, dos, qf):
    here, there = half(odd[0]), half(1 - odd[0])
    kv[0, here] = near_a[...]
    kv[0, there] = near_b[...]
    kv[1, here] = kv_mine[...]
    kv[1, there] = got[:, : 2 * PAIR]
    low = low_lanes((TOK, PAIR))
    zero = jnp.zeros((TOK, PAIR), BF16)
    for rows, part, first in ((here, q_mine, 0), (there, got, 2)):
        for i, out in enumerate((qs, dos)):
            x = part[:, (first + i) * PAIR : (first + i + 1) * PAIR]
            out[0, rows] = jnp.where(low, x, zero)
            out[1, rows] = jnp.where(low, zero, x)
    flip = flip_matrix(TOK)
    for b in range(REACH):
        back = mm(emb_t[:, span(REACH - 1 - b)], flip, NN).astype(BF16)
        erev[:HEAD_DIM, span(b)] = back
        erev[HEAD_DIM:, span(b)] = back
    flip = flip_matrix(ROWS)
    for h in range(HEADS):
        qf[h] = mm(flip, qs[h], NN).astype(BF16)


def main_body(odd, first, qs, dos, qf, erev, kv, far_a, far_b, far, d1, d0, gq, gemb, kv2):
    here, there = half(odd[0]), half(1 - odd[0])
    kv2[here] = far_a[...]
    kv2[there] = far_b[...]
    flip = flip_matrix(ROWS)
    row = lax.broadcasted_iota(jnp.int32, (ROWS, SPAN), 0)
    col = lax.broadcasted_iota(jnp.int32, (ROWS, SPAN), 1)
    ahead = col - row - 1
    valid = (ahead >= 0) & (ahead < BAND) & (col >= first[0])
    k = jnp.concatenate([x[:, :PAIR] for x in (kv2, kv.at[0], kv.at[1])], axis=0)
    v = jnp.concatenate([x[:, PAIR:] for x in (kv2, kv.at[0], kv.at[1])], axis=0)
    total = jnp.zeros((PAIR, BAND), F32)
    gk = jnp.zeros((PAIR, SPAN), F32)
    gv = jnp.zeros((PAIR, SPAN), F32)
    gq_parts, gqe_parts = [], []
    for h in range(HEADS):
        q, do = qs[h], dos[h]
        along = jnp.concatenate([mm(q, erev[...], NN), jnp.zeros((ROWS, ROWS), F32)], axis=1)
        s = (pltpu.roll(along, 1, 1, stride=1, stride_axis=0) + mm(q, k, NT)) * SCALE
        s = jnp.where(valid, s, -jnp.inf)
        dp = mm(do, v, NT)
        prob = jnp.exp(s - jnp.max(s, axis=1, keepdims=True))
        prob = prob * (1.0 / jnp.sum(prob, axis=1, keepdims=True))
        prob_b = prob.astype(BF16)
        delta = jnp.sum(prob_b.astype(F32) * dp, axis=1, keepdims=True)
        ds = (prob * (dp - delta) * SCALE).astype(BF16)
        dalong = pltpu.roll(mm(flip, ds, NN), BAND, 1, stride=1, stride_axis=0)[:, :BAND].astype(BF16)
        total = total + mm(qf[h], dalong, TN)
        gk = gk + mm(q, ds, TN)
        gv = gv + mm(do, prob_b, TN)
        gq_parts.append(mm(ds, k, NN))
        gqe_parts.append(mm(dalong, erev[...], NT))
    low = low_lanes((ROWS, PAIR))
    gqe = jnp.where(low, *gqe_parts)
    hi = gqe.astype(BF16)
    lo = (gqe - hi.astype(F32)).astype(BF16)
    gq[...] = (jnp.where(low, *gq_parts) + mm(flip, hi, NN) + mm(flip, lo, NN)).astype(BF16)
    for part, lanes in ((gk.T, slice(0, PAIR)), (gv.T, slice(PAIR, 2 * PAIR))):
        far[:, lanes] = part[:ROWS].astype(BF16)
        d1[:, lanes] = part[ROWS : 2 * ROWS]
        d0[:, lanes] = part[2 * ROWS :]
    total = total[:HEAD_DIM] + total[HEAD_DIM:]
    flip = flip_matrix(TOK)
    for b in range(REACH):
        block = mm(total[:, span(REACH - 1 - b)].astype(BF16), flip, NN)
        for d in range(HEAD_DIM // 8):
            gemb[d * REACH + b] = block[d * 8 : (d + 1) * 8].astype(BF16)


def sum_body(x, out):
    total = jnp.sum(x[...].astype(F32), axis=0, keepdims=True)
    out[...] = jnp.broadcast_to(total, out.shape).astype(BF16)


def place_body(x, out):
    for d in range(HEAD_DIM // 8):
        for b in range(REACH):
            out[d * 8 : (d + 1) * 8, span(b)] = x[d * REACH + b].astype(F32)


def add_body(got, d1, out):
    out[...] = (d1[...] + got[...].astype(F32)).astype(BF16)


def final_body(odd, got, d0, gq, keep, send):
    for rows, out in ((half(odd[0]), keep), (half(1 - odd[0]), send)):
        out[:, :PAIR] = gq[rows]
        out[:, PAIR:] = (d0[rows] + got[rows].astype(F32)).astype(BF16)


def unpack_body(odd, keep, got, *outs):
    swap = odd[0] > 0
    for i, out in enumerate(outs):
        lanes = slice(i * PAIR, (i + 1) * PAIR)
        a, b = keep[:, lanes], got[:, lanes]
        out[:, :PAIR] = jnp.where(swap, b, a)
        out[:, PAIR:] = jnp.where(swap, a, b)


SEQ = ("y", "zg", "zi")


def shift(x, steps, cross=False):
    n = lax.axis_size(SEQ)
    pairs = [(s, (s ^ 1 if cross else s) + steps) for s in range(n)]
    return near(lax.ppermute(x, SEQ, [(s, t) for s, t in pairs if 0 <= t < n]))


def exchange(x, axes):
    return lax.all_to_all(x, axes, 0, 0, tiled=True)


def local(query, key_rows, value_matrix_rows, grad_out, rel_embed):
    line, plane = ("zg", "zi"), ("y", "x", "core")
    here = lax.axis_index(SEQ)
    odd = (here & 1).reshape(1)
    first = (ROWS * jnp.maximum(BAND // ROWS - (here >> 1), 0)).reshape(1)
    sm, vm = pl.BlockSpec(memory_space=pltpu.SMEM), pl.BlockSpec(memory_space=pltpu.VMEM)

    def run(name, body, outs, scalars, *args, **kw):
        specs = [sm] * len(scalars) + [vm] * len(args)
        outs = call(body, outs, *scalars, *args, in_specs=specs, **kw)
        return [near(x) for x in outs] if name != "unpack" else outs

    half_unit, unit = ((TOK, 2 * PAIR), BF16, True), (ROWS, 2 * PAIR)
    kv_mine, kv_other, q_mine, other = run(
        "pack",
        pack_body,
        [half_unit] * 3 + [((TOK, 4 * PAIR), BF16, True)],
        [odd], key_rows, value_matrix_rows, query, grad_out,
    )
    got = shift(other, 0, True)
    near_a = shift(kv_mine, 2)
    near_b = shift(kv_other, 2, True)
    far_a = shift(near_a, 2)
    far_b = shift(near_b, 2)
    heads = ((HEADS, ROWS, PAIR), BF16, True)
    erev, kv, qs, dos, qf = run(
        "early",
        early_body,
        [((PAIR, BAND), BF16, True), ((2, ROWS, 2 * PAIR), BF16, True), heads, heads, heads],
        [odd], kv_mine, q_mine, got, near_a, near_b, rel_embed.T,
    )
    far, d1, d0, gq, gemb = run(
        "main",
        main_body,
        [(unit, BF16, True), (unit, F32, True), (unit, F32, True), ((ROWS, PAIR), BF16, True)]
        + [((lax.axis_size(plane), 8, 128), BF16, True)],
        [odd, first], qs, dos, qf, erev, kv, far_a, far_b,
        scratch_shapes=[pltpu.VMEM(unit, BF16)],
    )
    whole = exchange(gemb, plane)
    for axes in (line, plane):
        tiles = ((lax.axis_size(axes), 8, 128), BF16, True)
        (whole,) = call(sum_body, [tiles], near(whole))
        whole = exchange(whole, axes)
    (grad_embed_t,) = call(place_body, [((HEAD_DIM, BAND), F32, False)], near(whole), in_specs=[vm])
    back = shift(far, -2)
    (back,) = run("add", add_body, [(unit, BF16, True)], [], back, d1)
    back = shift(back, -2)
    third = ((TOK, 3 * PAIR), BF16, True)
    keep, send = run("final", final_body, [third] * 2, [odd], back, d0, gq)
    got = shift(send, 0, True)
    grads = run("unpack", unpack_body, [((TOK, 2 * PAIR), BF16, False)] * 3, [odd], keep, got)
    return (*grads, grad_embed_t.T)


def solution(mesh):
    fine = jax.sharding.Mesh(mesh.devices.reshape(DIMS), ("y", "zg", "zi", "x", "core"))
    rows = P(SEQ, ("x", "core"))
    return jax.shard_map(
        local,
        mesh=fine,
        in_specs=(rows, rows, rows, rows, P()),
        out_specs=(rows, rows, rows, P()),
        check_vma=False,
    )
```

```python
import jax
import jax.numpy as jnp
from jax import lax
from jax.experimental import pallas as pl
from jax.experimental.pallas import tpu as pltpu
from jax.sharding import PartitionSpec as P


HEAD_DIM = 64
BAND = 512
TOK = 128
REACH = BAND // TOK
HEADS = 2
PAIR = HEADS * HEAD_DIM
ROWS = 2 * TOK
SPAN = BAND + ROWS
DIMS = (4, 4, 4, 4, 2)
SCALE = HEAD_DIM ** (-0.5)
F32 = jnp.float32
BF16 = jnp.bfloat16
NN = ((1,), (0,))
NT = ((1,), (1,))
TN = ((0,), (0,))


def call(body, outs, *args, **kw):
    shapes = [pltpu.VMEM(s, d) if v else jax.ShapeDtypeStruct(s, d) for s, d, v in outs]
    return list(pl.pallas_call(body, out_shape=shapes, **kw)(*args))


def near(x):
    return pltpu.with_memory_space_constraint(x, pltpu.VMEM)


def mm(a, b, dims):
    return lax.dot_general(a, b, (dims, ((), ())), preferred_element_type=F32)


def span(block):
    return slice(block * TOK, (block + 1) * TOK)


def flip_matrix(count):
    row = lax.broadcasted_iota(jnp.int32, (count, count), 0)
    col = lax.broadcasted_iota(jnp.int32, (count, count), 1)
    return jnp.where(row + col == count - 1, 1.0, 0.0).astype(BF16)


def low_lanes(shape):
    return lax.broadcasted_iota(jnp.int32, shape, len(shape) - 1) < HEAD_DIM


def half(b):
    return pl.ds(pl.multiple_of(b * TOK, TOK), TOK)


def pick(take, x):
    low, high = x[:, :PAIR], x[:, PAIR:]
    return jnp.where(take, high, low), jnp.where(take, low, high)


def pack_body(odd, k, v, q, do, kv_mine, kv_other, q_mine, other):
    for i, x in enumerate((k, v, q, do)):
        a, b = pick(odd[0] > 0, x)
        other[:, i * PAIR : (i + 1) * PAIR] = b
        lanes = slice(i % 2 * PAIR, (i % 2 + 1) * PAIR)
        (kv_mine if i < 2 else q_mine)[:, lanes] = a
        if i < 2:
            kv_other[:, lanes] = b


def early_body(odd, kv_mine, q_mine, got, near_a, near_b, emb_t, erev, kv, qs, dos, qf):
    here, there = half(odd[0]), half(1 - odd[0])
    kv[0, here] = near_a[...]
    kv[0, there] = near_b[...]
    kv[1, here] = kv_mine[...]
    kv[1, there] = got[:, : 2 * PAIR]
    low = low_lanes((TOK, PAIR))
    zero = jnp.zeros((TOK, PAIR), BF16)
    for rows, part, first in ((here, q_mine, 0), (there, got, 2)):
        for i, out in enumerate((qs, dos)):
            x = part[:, (first + i) * PAIR : (first + i + 1) * PAIR]
            out[0, rows] = jnp.where(low, x, zero)
            out[1, rows] = jnp.where(low, zero, x)
    flip = flip_matrix(TOK)
    for b in range(REACH):
        back = mm(emb_t[:, span(REACH - 1 - b)], flip, NN).astype(BF16)
        erev[:HEAD_DIM, span(b)] = back
        erev[HEAD_DIM:, span(b)] = back
    flip = flip_matrix(ROWS)
    for h in range(HEADS):
        qf[h] = mm(flip, qs[h], NN).astype(BF16)


def main_body(odd, first, qs, dos, qf, erev, kv, far_a, far_b, far, d1, d0, gq, gemb, kv2):
    here, there = half(odd[0]), half(1 - odd[0])
    kv2[here] = far_a[...]
    kv2[there] = far_b[...]
    flip = flip_matrix(ROWS)
    row = lax.broadcasted_iota(jnp.int32, (ROWS, SPAN), 0)
    col = lax.broadcasted_iota(jnp.int32, (ROWS, SPAN), 1)
    ahead = col - row - 1
    valid = (ahead >= 0) & (ahead < BAND) & (col >= first[0])
    k = jnp.concatenate([x[:, :PAIR] for x in (kv2, kv.at[0], kv.at[1])], axis=0)
    v = jnp.concatenate([x[:, PAIR:] for x in (kv2, kv.at[0], kv.at[1])], axis=0)
    total = jnp.zeros((PAIR, BAND), F32)
    gk = jnp.zeros((PAIR, SPAN), F32)
    gv = jnp.zeros((PAIR, SPAN), F32)
    gq_parts, gqe_parts = [], []
    for h in range(HEADS):
        q, do = qs[h], dos[h]
        along = jnp.concatenate([mm(q, erev[...], NN), jnp.zeros((ROWS, ROWS), F32)], axis=1)
        s = (pltpu.roll(along, 1, 1, stride=1, stride_axis=0) + mm(q, k, NT)) * SCALE
        s = jnp.where(valid, s, -jnp.inf)
        dp = mm(do, v, NT)
        prob = jnp.exp(s - jnp.max(s, axis=1, keepdims=True))
        prob = prob * (1.0 / jnp.sum(prob, axis=1, keepdims=True))
        prob_b = prob.astype(BF16)
        delta = jnp.sum(prob_b.astype(F32) * dp, axis=1, keepdims=True)
        ds = (prob * (dp - delta) * SCALE).astype(BF16)
        dalong = pltpu.roll(mm(flip, ds, NN), BAND, 1, stride=1, stride_axis=0)[:, :BAND].astype(BF16)
        total = total + mm(qf[h], dalong, TN)
        gk = gk + mm(q, ds, TN)
        gv = gv + mm(do, prob_b, TN)
        gq_parts.append(mm(ds, k, NN))
        gqe_parts.append(mm(dalong, erev[...], NT))
    low = low_lanes((ROWS, PAIR))
    gqe = jnp.where(low, *gqe_parts)
    hi = gqe.astype(BF16)
    lo = (gqe - hi.astype(F32)).astype(BF16)
    gq[...] = (jnp.where(low, *gq_parts) + mm(flip, hi, NN) + mm(flip, lo, NN)).astype(BF16)
    for part, lanes in ((gk.T, slice(0, PAIR)), (gv.T, slice(PAIR, 2 * PAIR))):
        far[:, lanes] = part[:ROWS].astype(BF16)
        d1[:, lanes] = part[ROWS : 2 * ROWS]
        d0[:, lanes] = part[2 * ROWS :]
    total = total[:HEAD_DIM] + total[HEAD_DIM:]
    flip = flip_matrix(TOK)
    for b in range(REACH):
        block = mm(total[:, span(REACH - 1 - b)].astype(BF16), flip, NN)
        for d in range(HEAD_DIM // 8):
            gemb[d * REACH + b] = block[d * 8 : (d + 1) * 8].astype(BF16)


def sum_body(x, out):
    total = jnp.sum(x[...].astype(F32), axis=0, keepdims=True)
    out[...] = jnp.broadcast_to(total, out.shape).astype(BF16)


def add_body(got, d1, out):
    out[...] = (d1[...] + got[...].astype(F32)).astype(BF16)


def final_body(odd, got, d0, gq, keep, send):
    for rows, out in ((half(odd[0]), keep), (half(1 - odd[0]), send)):
        out[:, :PAIR] = gq[rows]
        out[:, PAIR:] = (d0[rows] + got[rows].astype(F32)).astype(BF16)


def unpack_body(odd, keep, got, *outs):
    swap = odd[0] > 0
    for i, out in enumerate(outs):
        lanes = slice(i * PAIR, (i + 1) * PAIR)
        a, b = keep[:, lanes], got[:, lanes]
        out[:, :PAIR] = jnp.where(swap, b, a)
        out[:, PAIR:] = jnp.where(swap, a, b)


SEQ = ("y", "zg", "zi")


def shift(x, steps, cross=False):
    n = lax.axis_size(SEQ)
    pairs = [(s, (s ^ 1 if cross else s) + steps) for s in range(n)]
    return near(lax.ppermute(x, SEQ, [(s, t) for s, t in pairs if 0 <= t < n]))


def exchange(x, axes):
    return lax.all_to_all(x, axes, 0, 0, tiled=True)


def local(query, key_rows, value_matrix_rows, grad_out, rel_embed):
    line, plane = ("zg", "zi"), ("y", "x", "core")
    here = lax.axis_index(SEQ)
    odd = (here & 1).reshape(1)
    first = (ROWS * jnp.maximum(BAND // ROWS - (here >> 1), 0)).reshape(1)
    sm, vm = pl.BlockSpec(memory_space=pltpu.SMEM), pl.BlockSpec(memory_space=pltpu.VMEM)

    def run(name, body, outs, scalars, *args, **kw):
        specs = [sm] * len(scalars) + [vm] * len(args)
        outs = call(body, outs, *scalars, *args, in_specs=specs, **kw)
        return [near(x) for x in outs] if name != "unpack" else outs

    half_unit, unit = ((TOK, 2 * PAIR), BF16, True), (ROWS, 2 * PAIR)
    kv_mine, kv_other, q_mine, other = run(
        "pack",
        pack_body,
        [half_unit] * 3 + [((TOK, 4 * PAIR), BF16, True)],
        [odd], key_rows, value_matrix_rows, query, grad_out,
    )
    got = shift(other, 0, True)
    near_a = shift(kv_mine, 2)
    near_b = shift(kv_other, 2, True)
    far_a = shift(near_a, 2)
    far_b = shift(near_b, 2)
    heads = ((HEADS, ROWS, PAIR), BF16, True)
    erev, kv, qs, dos, qf = run(
        "early",
        early_body,
        [((PAIR, BAND), BF16, True), ((2, ROWS, 2 * PAIR), BF16, True), heads, heads, heads],
        [odd], kv_mine, q_mine, got, near_a, near_b, rel_embed.T,
    )
    far, d1, d0, gq, gemb = run(
        "main",
        main_body,
        [(unit, BF16, True), (unit, F32, True), (unit, F32, True), ((ROWS, PAIR), BF16, True)]
        + [((lax.axis_size(plane), 8, 128), BF16, True)],
        [odd, first], qs, dos, qf, erev, kv, far_a, far_b,
        scratch_shapes=[pltpu.VMEM(unit, BF16)],
    )
    whole = exchange(gemb, plane)
    for axes in (line, plane):
        tiles = ((lax.axis_size(axes), 8, 128), BF16, True)
        (whole,) = call(sum_body, [tiles], near(whole))
        whole = exchange(whole, axes)
    grad_embed_t = whole.astype(F32).reshape(8, REACH, 8, 128).transpose(0, 2, 1, 3).reshape(HEAD_DIM, BAND)
    back = shift(far, -2)
    (back,) = run("add", add_body, [(unit, BF16, True)], [], back, d1)
    back = shift(back, -2)
    third = ((TOK, 3 * PAIR), BF16, True)
    keep, send = run("final", final_body, [third] * 2, [odd], back, d0, gq)
    got = shift(send, 0, True)
    grads = run("unpack", unpack_body, [((TOK, 2 * PAIR), BF16, False)] * 3, [odd], keep, got)
    return (*grads, grad_embed_t.T)


def solution(mesh):
    fine = jax.sharding.Mesh(mesh.devices.reshape(DIMS), ("y", "zg", "zi", "x", "core"))
    rows = P(SEQ, ("x", "core"))
    return jax.shard_map(
        local,
        mesh=fine,
        in_specs=(rows, rows, rows, rows, P()),
        out_specs=(rows, rows, rows, P()),
        check_vma=False,
    )
```
